768 devices in a mesh: seq: 48 (over z, x), tp: 16 (over y, core).
Axes of the slice: x: 4, y: 8, z: 12, core: 2. Of those that a mesh axis runs over, the one named last changes fastest.
Arguments:
- teacher_hidden: bfloat16 [6144, 4096], P('seq', 'tp'), may hold values from -6 to 6
- proj_weight: bfloat16 [4096, 3584], P('tp'), may hold values from -0.09375 to 0.09375
- student_in: bfloat16 [7680, 3584], P('seq'), may hold values from -6 to 6
- norm_gain: float32 [3584], replicated, may hold values from 0.25 to 1.75
- w_query: bfloat16 [3584, 4096], P(None, 'tp')
- w_keyval: bfloat16 [3584, 4096], P(None, 'tp')
- w_out: bfloat16 [4096, 3584], P('tp'), may hold values from -0.09375 to 0.09375
- row_offsets: int32 [48], P('seq'), may hold values from 0 to 5984, as said below
- row_counts: int32 [48], P('seq'), may hold values from 96 to 160, as said below
- doc_start: int32 [7680], P('seq'), may hold values from 0 to 159, as said below
Outputs:
- student_out: bfloat16 [7680, 3584], P('seq')
- grad_in: bfloat16 [7680, 3584], P(('seq', 'tp'))
The draws below stay inside these ranges and needn't reach their ends.
Inputs may be any that keep to these rules, and one draw needn't show every extreme that they name: Block s holds the tokens row_offsets[s] to row_offsets[s] + row_counts[s] - 1 in its first slots; row_offsets[0] = 0, for s >= 1 row_offsets[s] lies between s * 128 - 128 // 4 and s * 128 - 1, and row_offsets[s] + row_counts[s] = row_offsets[s + 1], the last block ending at 6144. `row_counts`: see row_offsets; some block holds 160 tokens and some 128 - 128 // 4. Within a block doc_start never falls, doc_start[p] <= p, documents lie whole in one block, and the slots from row_counts onward start a new document at row_counts.
All inputs are finite; a program needn't handle non-finite values.
Results may differ from the reference program's by a relative error of at most 0.028.
The reference program's roundings to bfloat16 on the way count: a program that leaves them out, or rounds other values in their place, can miss the bound.
Values may be sent and summed in bfloat16 or wider, within the bound.
No kernel may reach another device: no remote copies, remote signals or barrier semaphores. Data moves between devices by JAX's collectives and lax.ppermute only.
A program may use at most 64 MiB of HBM per device.

```python
import math
import jax
import jax.numpy as jnp
from jax import lax

DT = 4096
DS = 3584
HD = 128
QPK = 2
DOC_MEAN = 64
TOK_DEV = 128
SCAP = 160
KVH = 16
HQ = 32
TOKENS = 6144
SROWS = 7680
N_SEQ = 48
N_TP = 16


def layout_plan(key):
    first = jax.random.fold_in(key, 11)
    third = jax.random.fold_in(key, 13)
    quarter = TOK_DEV // 4
    index = jnp.arange(N_SEQ, dtype=jnp.int32)
    delta = jax.random.randint(first, (N_SEQ,), -quarter, 0)
    delta = jnp.where((index == 1) | (index == N_SEQ - 1), -quarter, delta)
    delta = jnp.where(index == 0, 0, delta)
    offsets = index * TOK_DEV + delta
    ends = jnp.concatenate([offsets[1:], jnp.full((1,), N_SEQ * TOK_DEV, jnp.int32)])
    counts = ends - offsets
    slots = jnp.arange(SCAP, dtype=jnp.int32)[None, :]
    flags = (jax.random.randint(third, (N_SEQ, SCAP), 0, DOC_MEAN) == 0) | (slots == 0) | (slots == counts[:, None])
    starts = lax.cummax(jnp.where(flags, slots, 0), axis=1)
    return (offsets.astype(jnp.int32), counts.astype(jnp.int32), starts.reshape(SROWS).astype(jnp.int32))


def attention_weights(key):
    qkey = jax.random.fold_in(key, 21)
    kkey = jax.random.fold_in(key, 22)
    wq = jax.random.normal(qkey, (DS, KVH, QPK, HD), jnp.float32) / math.sqrt(DS)
    wkv = jax.random.normal(kkey, (DS, KVH, 2, HD), jnp.float32) / math.sqrt(DS)
    return (wq.reshape(DS, HQ * HD).astype(jnp.bfloat16), wkv.reshape(DS, KVH * 2 * HD).astype(jnp.bfloat16))


def draw_w_query(key, part):
    return attention_weights(key)[0]


def draw_w_keyval(key, part):
    return attention_weights(key)[1]


def draw_row_offsets(key, part):
    return layout_plan(key)[0]


def draw_row_counts(key, part):
    return layout_plan(key)[1]


def draw_doc_start(key, part):
    return layout_plan(key)[2]


def level_of(own_key, extent, split, low, largest):
    def one(dim, shards_of):
        heights = jax.random.uniform(jax.random.fold_in(jax.random.fold_in(own_key, 6), dim), (shards_of,), jnp.float32, low / len(split), largest / len(split))
        return jnp.repeat(jnp.exp(heights), extent[dim] // shards_of).reshape((-1,) + (1,) * (len(extent) - dim - 1))

    gain = one(*split[0])
    for cut in split[1:]:
        gain = gain * one(*cut)
    return gain


def bell_draw(rng, shape, scale, limit, pieces=(), held_as=jnp.bfloat16):
    loudness = level_of(rng, shape, pieces, -0.22, 0.18) if pieces else 1.0
    result = jax.random.normal(rng, shape, jnp.float32) * scale * loudness
    return jnp.minimum(jnp.maximum(result, -limit), limit).astype(held_as)


def setup_inputs(seed: int = 0) -> dict:
    key_of = jax.random.split(jax.random.key(seed), 11)
    teacher_hidden = bell_draw(key_of[0], (TOKENS, DT), 1.0, 6.0, ((0, 48), (1, 16)))
    proj_weight = bell_draw(key_of[1], (DT, DS), DT ** -0.5, 0.09375, ((0, 16),))
    student_in = bell_draw(key_of[2], (SROWS, DS), 1.0, 6.0, ((0, 48),))
    norm_gain = jnp.clip(1.0 + 0.15 * jax.random.normal(key_of[3], (DS,), jnp.float32), 0.25, 1.75)
    w_query = draw_w_query(jax.random.fold_in(key_of[10], 71), 0)
    w_keyval = draw_w_keyval(jax.random.fold_in(key_of[10], 71), 0)
    w_out = bell_draw(key_of[6], (HQ * HD, DS), (HQ * HD) ** -0.5, 0.09375, ((0, 16),))
    row_offsets = draw_row_offsets(jax.random.fold_in(key_of[10], 71), 0)
    row_counts = draw_row_counts(jax.random.fold_in(key_of[10], 71), 0)
    doc_start = draw_doc_start(jax.random.fold_in(key_of[10], 71), 0)
    return {"teacher_hidden": teacher_hidden, "proj_weight": proj_weight, "student_in": student_in, "norm_gain": norm_gain, "w_query": w_query, "w_keyval": w_keyval, "w_out": w_out, "row_offsets": row_offsets, "row_counts": row_counts, "doc_start": doc_start}


epsilon = 1e-06

def student_block(rows, goal, count, starts, norm_gain, w_query, w_keyval, w_out):
    scale = 1.0 / math.sqrt(HD)
    xf = rows.astype(jnp.float32)
    inv = lax.rsqrt(lax.optimization_barrier(jnp.mean(xf * xf, axis=1, keepdims=True)) + epsilon)
    normed = (xf * inv * norm_gain).astype(jnp.bfloat16)
    query = jnp.dot(normed, w_query, preferred_element_type=jnp.float32).astype(jnp.bfloat16)
    keyval = jnp.dot(normed, w_keyval, preferred_element_type=jnp.float32).astype(jnp.bfloat16)
    qheads = query.reshape(SCAP, KVH, QPK, HD).astype(jnp.float32)
    kvheads = keyval.reshape(SCAP, KVH, 2, HD).astype(jnp.float32)
    keys = kvheads[:, :, 0, :]
    values = kvheads[:, :, 1, :]
    slots = jnp.arange(SCAP, dtype=jnp.int32)
    allowed = (slots[None, :] >= starts[:, None]) & (slots[None, :] <= slots[:, None])
    scores = jnp.einsum('pgeh,kgh->gepk', qheads, keys) * scale
    scores = jnp.where(allowed[None, None], scores, -jnp.inf)
    top = lax.optimization_barrier(jnp.max(scores, axis=-1, keepdims=True))
    expo = jnp.exp(scores - top)
    probs = expo / lax.optimization_barrier(jnp.sum(expo, axis=-1, keepdims=True))
    probs_b = probs.astype(jnp.bfloat16).astype(jnp.float32)
    attn = jnp.einsum('gepk,kgh->pgeh', probs_b, values).astype(jnp.bfloat16)
    attn = attn.reshape(SCAP, HQ * HD)
    width = QPK * HD
    branch = jnp.zeros((SCAP, DS), jnp.float32)
    for j in range(N_TP):
        piece = jnp.dot(attn[:, j * width:(j + 1) * width], w_out[j * width:(j + 1) * width], preferred_element_type=jnp.float32)
        branch = branch + piece.astype(jnp.bfloat16).astype(jnp.float32)
    student_out = (xf + branch).astype(jnp.bfloat16)
    yf = student_out.astype(jnp.float32)
    tf = goal.astype(jnp.float32)
    live = (slots < count).astype(jnp.float32)[:, None]
    asum = lax.optimization_barrier(jnp.sum(yf * yf, axis=1, keepdims=True)) + epsilon
    bsum = lax.optimization_barrier(jnp.sum(tf * tf, axis=1, keepdims=True)) + epsilon
    both = lax.rsqrt(asum * bsum)
    cosv = lax.optimization_barrier(jnp.sum(yf * tf, axis=1, keepdims=True)) * both
    dy = -math.sqrt(DS) * live * (tf * both - cosv * yf / asum)
    dy_b = dy.astype(jnp.bfloat16)
    d_attn = jnp.dot(dy_b, w_out.T, preferred_element_type=jnp.float32).astype(jnp.bfloat16)
    d_out = d_attn.reshape(SCAP, KVH, QPK, HD).astype(jnp.float32)
    d_values = jnp.einsum('gepk,pgeh->kgh', probs_b, d_out).astype(jnp.bfloat16)
    dprob = jnp.einsum('pgeh,kgh->gepk', d_out, values)
    dscore = probs * (dprob - lax.optimization_barrier(jnp.sum(dprob * probs, axis=-1, keepdims=True))) * scale
    dscore_b = dscore.astype(jnp.bfloat16).astype(jnp.float32)
    d_query = jnp.einsum('gepk,kgh->pgeh', dscore_b, keys).astype(jnp.bfloat16).reshape(SCAP, HQ * HD)
    d_keys = jnp.einsum('gepk,pgeh->kgh', dscore_b, qheads).astype(jnp.bfloat16)
    d_keyval = jnp.stack([d_keys, d_values], axis=2).reshape(SCAP, KVH * 2 * HD)
    d_normed = jnp.dot(d_query, w_query.T, preferred_element_type=jnp.float32) + jnp.dot(d_keyval, w_keyval.T, preferred_element_type=jnp.float32)
    upper = d_normed * norm_gain
    dx = inv * upper - xf * inv * inv * inv * lax.optimization_barrier(jnp.mean(upper * xf, axis=1, keepdims=True))
    grad_in = (dy + dx).astype(jnp.bfloat16)
    return (student_out, grad_in)

def reference(teacher_hidden, proj_weight, student_in, norm_gain, w_query, w_keyval, w_out, row_offsets, row_counts, doc_start):
    group = DT // N_TP
    total = jnp.zeros((TOKENS, DS), jnp.float32)
    for j in range(N_TP):
        piece = jnp.dot(teacher_hidden[:, j * group:(j + 1) * group], proj_weight[j * group:(j + 1) * group], preferred_element_type=jnp.float32)
        total = total + piece.astype(jnp.bfloat16).astype(jnp.float32)
    target = jnp.concatenate([total.astype(jnp.bfloat16), jnp.zeros((SCAP, DS), jnp.bfloat16)], axis=0)

    def one_block(index):
        rows = lax.dynamic_slice_in_dim(student_in, index * SCAP, SCAP, 0)
        goal = lax.dynamic_slice_in_dim(target, row_offsets[index].astype(jnp.int32), SCAP, 0)
        starts = lax.dynamic_slice_in_dim(doc_start, index * SCAP, SCAP, 0)
        return student_block(rows, goal, row_counts[index], starts, norm_gain, w_query, w_keyval, w_out)
    outputs, grads = lax.map(one_block, jnp.arange(N_SEQ, dtype=jnp.int32))
    return (outputs.reshape(SROWS, DS), grads.reshape(SROWS, DS))
```

```python
import math

import jax
import jax.numpy as jnp
from jax import lax
from jax.sharding import Mesh
from jax.sharding import PartitionSpec as P

HD = 128
QPK = 2
PAIR = [(0, 1), (1, 0)]


epsilon = 1e-06


def from_behind(block, axis, distance):
    devices = range(lax.axis_size(axis))
    route = [(i - distance, i) for i in devices if i - distance in devices]
    return lax.ppermute(block, axis, route)


def rows_of(array, first, count):
    return lax.dynamic_slice_in_dim(array, first, count, 0)


def sum_blocks(part, core, cols):
    half = part.shape[0] // 2
    width = part.shape[1]
    mine = rows_of(part, core * half, half).astype(jnp.float32)
    other = lax.ppermute(rows_of(part, (1 - core) * half, half), "core", PAIR)
    chip = (mine + other.astype(jnp.float32)).astype(jnp.bfloat16)
    bands = 8 // cols
    blocks = chip.reshape(bands, half // bands, cols, width // cols).transpose(0, 2, 1, 3)
    blocks = blocks.reshape(8, half // bands, width // cols)
    got = lax.all_to_all(blocks, "y", 0, 0)
    return jnp.sum(got.astype(jnp.float32), axis=0)


def gather_blocks(block, core, cols):
    bands = 8 // cols
    high, wide = block.shape
    got = lax.all_to_all(jnp.broadcast_to(block[None], (8, high, wide)), "y", 0, 0)
    half = got.reshape(bands, cols, high, wide).transpose(0, 2, 1, 3).reshape(bands * high, cols * wide)
    other = lax.ppermute(half, "core", PAIR)
    first = jnp.where(core == 0, half, other)
    second = jnp.where(core == 0, other, half)
    return jnp.concatenate([first, second], axis=0)


def body(
    teacher_hidden,
    proj_weight,
    student_in,
    norm_gain,
    w_query,
    w_keyval,
    w_out,
    row_offsets,
    row_counts,
    doc_start,
):
    scale = 1.0 / math.sqrt(HD)
    tokens_here = teacher_hidden.shape[0]
    quarter = tokens_here // 4
    slots_here = student_in.shape[0]
    width = student_in.shape[1]
    cols = 4
    core = lax.axis_index("core")
    ypos = lax.axis_index("y")
    start = row_offsets[0] - lax.axis_index("seq") * tokens_here + quarter
    count = row_counts[0]
    earlier = from_behind(teacher_hidden[tokens_here - quarter :], "seq", 1)
    blank = jnp.zeros((quarter, teacher_hidden.shape[1]), jnp.bfloat16)
    window = jnp.concatenate([earlier, teacher_hidden, blank], axis=0)
    window = lax.dynamic_slice_in_dim(window, start, slots_here, 0)
    goal_part = jnp.dot(window, proj_weight, preferred_element_type=jnp.float32).astype(
        jnp.bfloat16
    )
    goal_own = sum_blocks(goal_part, core, cols).astype(jnp.bfloat16)
    goal = gather_blocks(goal_own, core, cols)
    xf = student_in.astype(jnp.float32)
    inv = lax.rsqrt(jnp.mean(xf * xf, axis=1, keepdims=True) + epsilon)
    normed = (xf * inv * norm_gain).astype(jnp.bfloat16)
    query = (
        jnp.dot(normed, w_query, preferred_element_type=jnp.float32)
        .astype(jnp.bfloat16)
        .reshape(slots_here, QPK, HD)
    )
    keyval = (
        jnp.dot(normed, w_keyval, preferred_element_type=jnp.float32)
        .astype(jnp.bfloat16)
        .reshape(slots_here, 2, HD)
    )
    keys = keyval[:, 0, :]
    values = keyval[:, 1, :]
    slots = jnp.arange(slots_here, dtype=jnp.int32)
    allowed = (slots[None, :] >= doc_start[:, None]) & (slots[None, :] <= slots[:, None])
    scores = jnp.einsum("peh,kh->epk", query, keys, preferred_element_type=jnp.float32) * scale
    scores = jnp.where(allowed[None], scores, -jnp.inf)
    top = jnp.max(scores, axis=-1, keepdims=True)
    expo = jnp.exp(scores - top)
    probs = expo / jnp.sum(expo, axis=-1, keepdims=True)
    probs_b = probs.astype(jnp.bfloat16)
    attn = jnp.einsum("epk,kh->peh", probs_b, values, preferred_element_type=jnp.float32).astype(
        jnp.bfloat16
    )
    attn = attn.reshape(slots_here, QPK * HD)
    branch_part = jnp.dot(attn, w_out, preferred_element_type=jnp.float32).astype(jnp.bfloat16)
    high = slots_here // (2 * (8 // cols))
    x_block = lax.dynamic_slice(
        student_in,
        (core * (slots_here // 2) + (ypos // cols) * high, (ypos % cols) * (width // cols)),
        (high, width // cols),
    )
    y_own = (x_block.astype(jnp.float32) + sum_blocks(branch_part, core, cols)).astype(jnp.bfloat16)
    student_out = gather_blocks(y_own, core, cols)
    yf = student_out.astype(jnp.float32)
    tf = goal.astype(jnp.float32)
    live = (slots < count).astype(jnp.float32)[:, None]
    asum = jnp.sum(yf * yf, axis=1, keepdims=True) + epsilon
    bsum = jnp.sum(tf * tf, axis=1, keepdims=True) + epsilon
    both = lax.rsqrt(asum * bsum)
    cosv = jnp.sum(yf * tf, axis=1, keepdims=True) * both
    dy = -math.sqrt(width) * live * (tf * both - cosv * yf / asum)
    dy_b = dy.astype(jnp.bfloat16)
    d_attn = lax.dot_general(
        dy_b, w_out, (((1,), (1,)), ((), ())), preferred_element_type=jnp.float32
    ).astype(jnp.bfloat16)
    d_out = d_attn.reshape(slots_here, QPK, HD)
    d_values = jnp.einsum("epk,peh->kh", probs_b, d_out, preferred_element_type=jnp.float32).astype(
        jnp.bfloat16
    )
    dprob = jnp.einsum("peh,kh->epk", d_out, values, preferred_element_type=jnp.float32)
    dscore = probs * (dprob - jnp.sum(dprob * probs, axis=-1, keepdims=True)) * scale
    dscore_b = dscore.astype(jnp.bfloat16)
    d_query = jnp.einsum("epk,kh->peh", dscore_b, keys, preferred_element_type=jnp.float32).astype(
        jnp.bfloat16
    )
    d_query = d_query.reshape(slots_here, QPK * HD)
    d_keys = jnp.einsum("epk,peh->kh", dscore_b, query, preferred_element_type=jnp.float32).astype(
        jnp.bfloat16
    )
    d_keyval = jnp.stack([d_keys, d_values], axis=1).reshape(slots_here, 2 * HD)
    total = lax.dot_general(
        d_query, w_query, (((1,), (1,)), ((), ())), preferred_element_type=jnp.float32
    )
    own_rows = slots_here // 16
    part = (
        (
            total
            + lax.dot_general(
                d_keyval, w_keyval, (((1,), (1,)), ((), ())), preferred_element_type=jnp.float32
            )
        )
        .astype(jnp.bfloat16)
        .reshape(8, 2, own_rows * width // HD, HD)
    )
    mine = lax.dynamic_index_in_dim(part, core, 1, keepdims=False).astype(jnp.float32)
    other = lax.ppermute(
        lax.dynamic_index_in_dim(part, 1 - core, 1, keepdims=False), "core", PAIR
    ).astype(jnp.float32)
    got = lax.all_to_all((mine + other).astype(jnp.bfloat16), "y", 0, 0)
    d_normed = jnp.sum(got.astype(jnp.float32), axis=0).reshape(own_rows, width)
    first_row = (ypos * 2 + core) * own_rows
    x_own = lax.dynamic_slice_in_dim(xf, first_row, own_rows, 0)
    inv_own = lax.dynamic_slice_in_dim(inv, first_row, own_rows, 0)
    dy_own = lax.dynamic_slice_in_dim(dy, first_row, own_rows, 0)
    upper = d_normed * norm_gain
    dx = inv_own * upper - x_own * inv_own * inv_own * inv_own * jnp.mean(
        upper * x_own, axis=1, keepdims=True
    )
    grad_in = (dy_own + dx).astype(jnp.bfloat16)
    return (student_out, grad_in)


def solution(mesh):
    seqs, tps = mesh.devices.shape
    split = Mesh(mesh.devices.reshape(seqs, tps // 2, 2), ("seq", "y", "core"))
    tp = ("y", "core")
    in_specs = (
        P("seq", tp),
        P(tp, None),
        P("seq", None),
        P(),
        P(None, tp),
        P(None, tp),
        P(tp, None),
        P("seq"),
        P("seq"),
        P("seq"),
    )
    out_specs = (P("seq", None), P(("seq", "y", "core"), None))
    return jax.shard_map(body, mesh=split, in_specs=in_specs, out_specs=out_specs, check_vma=False)
```

```python
import math

import jax
import jax.numpy as jnp
from jax import lax
from jax.experimental import pallas as pl
from jax.experimental.pallas import tpu as pltpu
from jax.sharding import Mesh
from jax.sharding import PartitionSpec as P

HD = 128
QPK = 2
PAIR = [(0, 1), (1, 0)]
COLS = 4
TP = ("y", "core")
CUT = 24

epsilon = 1e-06

VMEM = pl.BlockSpec(memory_space=pltpu.VMEM)
SMEM = pl.BlockSpec(memory_space=pltpu.SMEM)
ANY = pl.BlockSpec(memory_space=pl.ANY)
F32 = jnp.float32
BF16 = jnp.bfloat16


def shape(dims, dtype):
    return jax.ShapeDtypeStruct(dims, dtype)


def nt(a, b):
    return lax.dot_general(a, b, (((1,), (1,)), ((), ())), preferred_element_type=F32)


def tn(a, b):
    return lax.dot_general(a, b, (((0,), (0,)), ((), ())), preferred_element_type=F32)


def nn(a, b):
    return jnp.dot(a, b, preferred_element_type=F32)


def emit_blocks(core, lhs_ref, weight_ref, mine_ref, send_ref):
    half = lhs_ref.shape[0] // 2
    high, wide = mine_ref.shape[1:]
    first = lhs_ref[pl.ds(pl.multiple_of(core * half, 16), half), :]
    second = lhs_ref[pl.ds(pl.multiple_of((1 - core) * half, 16), half), :]
    lhs = jnp.concatenate([first, second], axis=0)
    for j in range(COLS):
        out = nn(lhs, weight_ref[:, j * wide : (j + 1) * wide])
        for i in range(2):
            mine_ref[i * COLS + j] = out[i * high : (i + 1) * high].astype(BF16)
            send_ref[i * COLS + j] = out[half + i * high : half + (i + 1) * high].astype(BF16)


def goal_kernel(core_ref, rows_ref, weight_ref, mine_ref, send_ref):
    emit_blocks(core_ref[0], rows_ref, weight_ref, mine_ref, send_ref)


def forward_kernel(
    core_ref,
    x_ref,
    gain_ref,
    starts_ref,
    w_query_hbm,
    w_keyval_hbm,
    w_out_hbm,
    query_ref,
    keyval_ref,
    probs_ref,
    mine_ref,
    send_ref,
    w_query,
    w_keyval,
    w_out,
    attn_ref,
    sems,
):
    loads = [
        pltpu.make_async_copy(source, target, sems.at[n])
        for n, (source, target) in enumerate(
            ((w_query_hbm, w_query), (w_keyval_hbm, w_keyval), (w_out_hbm, w_out))
        )
    ]
    for load in loads:
        load.start()
    slots = x_ref.shape[0]
    xf = x_ref[...].astype(F32)
    inv = lax.rsqrt(jnp.mean(xf * xf, axis=1, keepdims=True) + epsilon)
    normed = (xf * inv * gain_ref[...]).astype(BF16)
    loads[0].wait()
    query = nn(normed, w_query[...]).astype(BF16)
    query_ref[...] = query
    loads[1].wait()
    keyval = nn(normed, w_keyval[...]).astype(BF16)
    keyval_ref[...] = keyval
    keys = keyval[:, :HD]
    values = keyval[:, HD:]
    row = lax.broadcasted_iota(jnp.int32, (slots, slots), 0)
    col = lax.broadcasted_iota(jnp.int32, (slots, slots), 1)
    allowed = (col >= starts_ref[...]) & (col <= row)
    for e in range(QPK):
        scores = nt(query[:, e * HD : (e + 1) * HD], keys) * (1.0 / math.sqrt(HD))
        scores = jnp.where(allowed, scores, -jnp.inf)
        expo = jnp.exp(scores - jnp.max(scores, axis=1, keepdims=True))
        probs = expo / jnp.sum(expo, axis=1, keepdims=True)
        probs_ref[e] = probs
        attn_ref[:, e * HD : (e + 1) * HD] = nn(probs.astype(BF16), values).astype(BF16)
    loads[2].wait()
    emit_blocks(core_ref[0], attn_ref, w_out, mine_ref, send_ref)


def total_kernel(got_ref, x_ref, out_ref):
    total = x_ref[...].astype(F32)
    branch = got_ref[0].astype(F32)
    for n in range(1, got_ref.shape[0]):
        branch = branch + got_ref[n].astype(F32)
    total = (total + branch).astype(BF16)
    for n in range(out_ref.shape[0]):
        out_ref[n] = total


def backward_kernel(
    core_ref,
    count_ref,
    own_ref,
    other_ref,
    top_ref,
    bottom_ref,
    probs_ref,
    query_ref,
    keyval_ref,
    w_out_hbm,
    w_query_hbm,
    w_keyval_hbm,
    student_ref,
    dy_hbm,
    mine_ref,
    send_ref,
    w_out,
    w_query,
    w_keyval,
    dy_ref,
    dyb_ref,
    grads_ref,
    sems,
):
    loads = [
        pltpu.make_async_copy(source, target, sems.at[n])
        for n, (source, target) in enumerate(
            ((w_out_hbm, w_out), (w_query_hbm, w_query), (w_keyval_hbm, w_keyval))
        )
    ]
    for load in loads:
        load.start()
    core = core_ref[0]
    count = count_ref[0]
    slots, width = student_ref.shape
    high, wide = own_ref.shape[1:]
    for c in range(2):
        for i in range(2):
            y, t = [], []
            for j in range(COLS):
                n = i * COLS + j
                block = jnp.where(core == c, own_ref[n].astype(F32), other_ref[n].astype(F32))
                y.append(block)
                t.append(
                    jnp.concatenate(
                        [top_ref[2 * n + c].astype(F32), bottom_ref[2 * n + c].astype(F32)], axis=0
                    )
                )
            asum = sum(jnp.sum(a * a, axis=1, keepdims=True) for a in y) + epsilon
            bsum = sum(jnp.sum(a * a, axis=1, keepdims=True) for a in t) + epsilon
            dots = sum(jnp.sum(a * b, axis=1, keepdims=True) for a, b in zip(y, t))
            both = lax.rsqrt(asum * bsum)
            first = (2 * c + i) * high
            live = (
                lax.broadcasted_iota(jnp.int32, (high, 1), 0) + first < count
            ).astype(F32)
            factor = -math.sqrt(width) * live
            t_scale = factor * both
            y_scale = factor * (dots * both) / asum
            for j in range(COLS):
                dy = t[j] * t_scale - y[j] * y_scale
                where = (slice(first, first + high), slice(j * wide, (j + 1) * wide))
                student_ref[where] = y[j].astype(BF16)
                dy_ref[where] = dy
                dyb_ref[where] = dy.astype(BF16)
    store = pltpu.make_async_copy(dy_ref, dy_hbm, sems.at[3])
    store.start()
    loads[0].wait()
    d_attn = nt(dyb_ref[...], w_out[...]).astype(BF16)
    keys = keyval_ref[:, :HD]
    values = keyval_ref[:, HD:]
    d_keys = d_values = None
    for e in range(QPK):
        head = slice(e * HD, (e + 1) * HD)
        d_out = d_attn[:, head]
        probs = probs_ref[e]
        d_value = tn(probs.astype(BF16), d_out)
        dprob = nt(d_out, values)
        dscore = probs * (dprob - jnp.sum(dprob * probs, axis=1, keepdims=True))
        dscore = (dscore * (1.0 / math.sqrt(HD))).astype(BF16)
        grads_ref[:, head] = nn(dscore, keys).astype(BF16)
        d_key = tn(dscore, query_ref[:, head])
        d_keys = d_key if d_keys is None else d_keys + d_key
        d_values = d_value if d_values is None else d_values + d_value
    grads_ref[:, QPK * HD : (QPK + 1) * HD] = d_keys.astype(BF16)
    grads_ref[:, (QPK + 1) * HD :] = d_values.astype(BF16)
    half = slots // 2
    row = lax.broadcasted_iota(jnp.int32, (slots, slots), 0)
    col = lax.broadcasted_iota(jnp.int32, (slots, slots), 1)
    sent = (row >= half).astype(jnp.int32)
    place = row - half * sent
    parity = core + sent - 2 * core * sent
    late = (place >= 64).astype(jnp.int32)
    early_row = 20 * (place >> 3) + (place & 7)
    late_row = 20 * ((place - 64) >> 1) + 8 + (place & 1)
    source = early_row + late * (late_row - early_row) + 10 * parity
    pick = (col == source).astype(BF16)
    rows = nn(pick, grads_ref[...]).astype(BF16)
    loads[1].wait()
    loads[2].wait()
    sub = lax.broadcasted_iota(jnp.int32, (8, HD), 0) >> 1
    for j in range(width // (4 * HD)):
        span = slice(j * 4 * HD, (j + 1) * 4 * HD)
        part = nt(rows[:, : QPK * HD], w_query[span, :]) + nt(rows[:, QPK * HD :], w_keyval[span, :])
        for h, ref in ((0, mine_ref), (1, send_ref)):
            base = h * half
            for k in range(4):
                lane = slice(k * HD, (k + 1) * HD)
                at = 8 * (4 * j + k)
                for n in range(8):
                    ref[n, at : at + 8, :] = part[base + 8 * n : base + 8 * n + 8, lane].astype(BF16)
            for g in range(2):
                low = base + 64 + 8 * g
                tiles = [part[low : low + 8, k * HD : (k + 1) * HD] for k in range(4)]
                for i in range(4):
                    tile = None
                    for k in range(4):
                        turned = pltpu.roll(tiles[k], (2 * k - 2 * i) % 8, 0) if k != i else tiles[k]
                        tile = turned if tile is None else jnp.where(sub == k, turned, tile)
                    at = 224 + 8 * j
                    ref[4 * g + i, at : at + 8, :] = tile.astype(BF16)
    store.wait()


def final_kernel(got_ref, x_ref, dy_ref, gain_ref, out_ref, rows_ref):
    total = got_ref[0].astype(F32)
    for n in range(1, got_ref.shape[0]):
        total = total + got_ref[n].astype(F32)
    for t in range(28):
        lane = slice(t * HD, (t + 1) * HD)
        rows_ref[0:8, lane] = total[8 * t : 8 * t + 8]
        at = 224 + 2 * t
        rows_ref[8:10, lane] = total[at : at + 2]
    x = x_ref[...].astype(F32)
    inv = lax.rsqrt(jnp.mean(x * x, axis=1, keepdims=True) + epsilon)
    upper = rows_ref[0:10, :] * gain_ref[...]
    dx = inv * upper - x * (inv * inv * inv) * jnp.mean(upper * x, axis=1, keepdims=True)
    out_ref[...] = (dy_ref[...] + dx).astype(BF16)


def from_behind(block, axis, distance):
    devices = range(lax.axis_size(axis))
    route = [(i - distance, i) for i in devices if i - distance in devices]
    return lax.ppermute(block, axis, route)


def swap(block):
    return lax.ppermute(block, "core", PAIR)


def spread(mine, send):
    other = swap(send)
    chip = (mine.astype(F32) + other.astype(F32)).astype(BF16)
    return lax.all_to_all(chip, "y", 0, 0)


def body(
    teacher_hidden,
    proj_weight,
    student_in,
    norm_gain,
    w_query,
    w_keyval,
    w_out,
    row_offsets,
    row_counts,
    doc_start,
):
    tokens_here = teacher_hidden.shape[0]
    quarter = tokens_here // 4
    slots, width = student_in.shape
    high, wide = slots // 4, width // COLS
    core = lax.axis_index("core")
    ypos = lax.axis_index("y")
    core_s = core.astype(jnp.int32).reshape(1)
    start = row_offsets[0] - lax.axis_index("seq") * tokens_here + quarter
    blocks = shape((8, high, wide), BF16)
    with jax.named_scope("shift"):
        earlier = from_behind(teacher_hidden[tokens_here - quarter :], "seq", 1)
    blank = jnp.zeros((quarter, teacher_hidden.shape[1]), BF16)
    window = jnp.concatenate([earlier, teacher_hidden, blank], axis=0)
    window = lax.dynamic_slice_in_dim(window, start, slots, 0)
    goal_mine, goal_send = pl.pallas_call(
        goal_kernel,
        out_shape=(blocks, blocks),
        in_specs=[SMEM, VMEM, VMEM],
        out_specs=(VMEM, VMEM),
        name="goal",
    )(core_s, window, proj_weight)
    with jax.named_scope("rsa"):
        goal_got = spread(goal_mine, goal_send)
    gain = norm_gain.reshape(1, width)
    query, keyval, probs, mine, send = pl.pallas_call(
        forward_kernel,
        out_shape=(
            shape((slots, QPK * HD), BF16),
            shape((slots, 2 * HD), BF16),
            shape((QPK, slots, slots), F32),
            blocks,
            blocks,
        ),
        in_specs=[SMEM, VMEM, VMEM, VMEM, ANY, ANY, ANY],
        out_specs=(VMEM,) * 5,
        scratch_shapes=[
            pltpu.VMEM(w_query.shape, BF16),
            pltpu.VMEM(w_keyval.shape, BF16),
            pltpu.VMEM(w_out.shape, BF16),
            pltpu.VMEM((slots, QPK * HD), BF16),
            pltpu.SemaphoreType.DMA((3,)),
        ],
        name="forward",
    )(core_s, student_in, gain, doc_start.reshape(slots, 1), w_query, w_keyval, w_out)
    with jax.named_scope("rsb"):
        branch_got = spread(mine, send)
    goal_own = jnp.sum(goal_got.astype(F32), axis=0).astype(BF16)
    with jax.named_scope("agt1"):
        goal_top = lax.all_gather(goal_own[:CUT], TP)
    with jax.named_scope("agt2"):
        goal_bottom = lax.all_gather(goal_own[CUT:], TP)
    x_block = lax.dynamic_slice(
        student_in,
        (core * (slots // 2) + (ypos // COLS) * high, (ypos % COLS) * wide),
        (high, wide),
    )
    y_own = pl.pallas_call(
        total_kernel, out_shape=blocks, in_specs=[VMEM, VMEM], out_specs=VMEM, name="total"
    )(branch_got, x_block)
    with jax.named_scope("agy"):
        y_half = lax.all_to_all(y_own, "y", 0, 0)
    y_other = swap(y_half)
    pieces = shape((8, slots // 16 * (width // HD), HD), BF16)
    student_out, dy, mine, send = pl.pallas_call(
        backward_kernel,
        out_shape=(shape((slots, width), BF16), shape((slots, width), F32), pieces, pieces),
        in_specs=[SMEM, SMEM] + [VMEM] * 7 + [ANY] * 3,
        out_specs=(VMEM, ANY, VMEM, VMEM),
        scratch_shapes=[
            pltpu.VMEM(w_out.shape, BF16),
            pltpu.VMEM(w_query.shape, BF16),
            pltpu.VMEM(w_keyval.shape, BF16),
            pltpu.VMEM((slots, width), F32),
            pltpu.VMEM((slots, width), BF16),
            pltpu.VMEM((slots, (QPK + 2) * HD), BF16),
            pltpu.SemaphoreType.DMA((4,)),
        ],
        name="backward",
    )(
        core_s,
        row_counts,
        y_half,
        y_other,
        goal_top,
        goal_bottom,
        probs,
        query,
        keyval,
        w_out,
        w_query,
        w_keyval,
    )
    with jax.named_scope("rsd"):
        got = spread(mine, send)
    own_rows = slots // 16
    first_row = (ypos * 2 + core) * own_rows
    x_own = lax.dynamic_slice_in_dim(student_in, first_row, own_rows, 0)
    dy_own = lax.dynamic_slice_in_dim(dy, first_row, own_rows, 0)
    grad_in = pl.pallas_call(
        final_kernel,
        out_shape=shape((own_rows, width), BF16),
        in_specs=[VMEM] * 4,
        out_specs=VMEM,
        scratch_shapes=[pltpu.VMEM((16, width), F32)],
        name="final",
    )(got, x_own, dy_own, gain)
    return (student_out, grad_in)


def solution(mesh):
    seqs, tps = mesh.devices.shape
    split = Mesh(mesh.devices.reshape(seqs, tps // 2, 2), ("seq",) + TP)
    in_specs = (
        P("seq", TP),
        P(TP, None),
        P("seq", None),
        P(),
        P(None, TP),
        P(None, TP),
        P(TP, None),
        P("seq"),
        P("seq"),
        P("seq"),
    )
    out_specs = (P("seq", None), P(("seq",) + TP, None))
    return jax.shard_map(body, mesh=split, in_specs=in_specs, out_specs=out_specs, check_vma=False)
```

```python
import math

import jax
import jax.numpy as jnp
from jax import lax
from jax.experimental import pallas as pl
from jax.experimental.pallas import tpu as pltpu
from jax.sharding import Mesh
from jax.sharding import PartitionSpec as P

HD = 128
QPK = 2
PAIR = [(0, 1), (1, 0)]
COLS = 4
TP = ("y", "core")

epsilon = 1e-06

VMEM = pl.BlockSpec(memory_space=pltpu.VMEM)
SMEM = pl.BlockSpec(memory_space=pltpu.SMEM)
HBM = pl.BlockSpec(memory_space=pltpu.HBM)
F32 = jnp.float32
BF16 = jnp.bfloat16


def near(array):
    return pltpu.with_memory_space_constraint(array, pltpu.VMEM)


def shape(dims, dtype):
    return jax.ShapeDtypeStruct(dims, dtype)


def nt(a, b):
    return lax.dot_general(a, b, (((1,), (1,)), ((), ())), preferred_element_type=F32)


def tn(a, b):
    return lax.dot_general(a, b, (((0,), (0,)), ((), ())), preferred_element_type=F32)


def nn(a, b):
    return jnp.dot(a, b, preferred_element_type=F32)


def emit_blocks(core, lhs_ref, weight_ref, mine_ref, send_ref, loads=()):
    half = lhs_ref.shape[0] // 2
    high, wide = mine_ref.shape[1:]
    first = lhs_ref[pl.ds(pl.multiple_of(core * half, 16), half), :]
    second = lhs_ref[pl.ds(pl.multiple_of((1 - core) * half, 16), half), :]
    lhs = jnp.concatenate([first, second], axis=0)
    for j in range(COLS):
        if loads:
            loads[j].wait()
        out = nn(lhs, weight_ref[:, j * wide : (j + 1) * wide])
        for i in range(2):
            mine_ref[i * COLS + j] = out[i * high : (i + 1) * high].astype(BF16)
            send_ref[i * COLS + j] = out[half + i * high : half + (i + 1) * high].astype(BF16)


def goal_kernel(core_ref, rows_ref, weight_hbm, mine_ref, send_ref, weight_ref, sems):
    wide = mine_ref.shape[2]
    loads = []
    for j in range(COLS):
        span = slice(j * wide, (j + 1) * wide)
        load = pltpu.make_async_copy(weight_hbm.at[:, span], weight_ref.at[:, span], sems.at[j])
        load.start()
        loads.append(load)
    emit_blocks(core_ref[0], rows_ref, weight_ref, mine_ref, send_ref, loads)


def pair_kernel(mine_ref, other_ref, out_hbm, sum_ref, sems):
    stores = []
    for n in range(out_hbm.shape[0]):
        sum_ref[n] = (mine_ref[n].astype(F32) + other_ref[n].astype(F32)).astype(BF16)
        stores.append(pltpu.make_async_copy(sum_ref.at[n], out_hbm.at[n], sems.at[n]))
        stores[n].start()
    for store in stores:
        store.wait()


def align_kernel(start_ref, own_ref, earlier_ref, out_ref):
    slots = out_ref.shape[0]
    wide = own_ref.shape[2]
    row = lax.broadcasted_iota(jnp.int32, (slots, slots), 0)
    col = lax.broadcasted_iota(jnp.int32, (slots, slots), 1)
    pick = (col == row + start_ref[0]).astype(BF16)
    for j in range(COLS):
        bands = [earlier_ref[j]]
        for c in range(2):
            for i in range(2):
                bands.append(own_ref[2 * (i * COLS + j) + c])
        rows = jnp.concatenate(bands, axis=0)
        out_ref[:, j * wide : (j + 1) * wide] = nn(pick, rows).astype(BF16)


def direction(y, t, live, width):
    asum = sum(jnp.sum(a * a, axis=1, keepdims=True) for a in y) + epsilon
    bsum = sum(jnp.sum(a * a, axis=1, keepdims=True) for a in t) + epsilon
    dots = sum(jnp.sum(a * b, axis=1, keepdims=True) for a, b in zip(y, t))
    both = lax.rsqrt(asum * bsum)
    factor = -math.sqrt(width) * live
    return factor * both, factor * (dots * both) / asum


def finish_kernel(
    core_ref, first_ref, count_ref, own_ref, other_ref, goal_ref, x_ref, student_ref, dy_ref, x_own_ref
):
    core = core_ref[0]
    slots, width = student_ref.shape
    high, wide = own_ref.shape[1:]
    for c in range(2):
        for i in range(2):
            first = (2 * c + i) * high
            for j in range(COLS):
                n = i * COLS + j
                block = jnp.where(core == c, own_ref[n].astype(F32), other_ref[n].astype(F32))
                student_ref[first : first + high, j * wide : (j + 1) * wide] = block.astype(BF16)
    own_rows = dy_ref.shape[0]
    row = lax.broadcasted_iota(jnp.int32, (16, slots), 0) + first_ref[0]
    col = lax.broadcasted_iota(jnp.int32, (16, slots), 1)
    pick = (col == row).astype(BF16)
    y = nn(pick, student_ref[...])
    t = nn(pick, goal_ref[...])
    x_own_ref[...] = nn(pick, x_ref[...])[:own_rows]
    place = lax.broadcasted_iota(jnp.int32, (16, 1), 0) + first_ref[0]
    t_scale, y_scale = direction([y], [t], (place < count_ref[0]).astype(F32), width)
    dy_ref[...] = (t * t_scale - y * y_scale)[:own_rows]


def forward_kernel(
    core_ref,
    x_ref,
    gain_ref,
    starts_ref,
    w_query_hbm,
    w_keyval_hbm,
    w_out_hbm,
    query_ref,
    keyval_ref,
    probs_ref,
    mine_ref,
    send_ref,
    w_query,
    w_keyval,
    w_out,
    attn_ref,
    sems,
):
    loads = [
        pltpu.make_async_copy(source, target, sems.at[n])
        for n, (source, target) in enumerate(
            ((w_query_hbm, w_query), (w_keyval_hbm, w_keyval), (w_out_hbm, w_out))
        )
    ]
    for load in loads:
        load.start()
    slots = x_ref.shape[0]
    xf = x_ref[...].astype(F32)
    inv = lax.rsqrt(jnp.mean(xf * xf, axis=1, keepdims=True) + epsilon)
    normed = (xf * inv * gain_ref[...].reshape(1, xf.shape[1])).astype(BF16)
    loads[0].wait()
    query = nn(normed, w_query[...]).astype(BF16)
    query_ref[...] = query
    loads[1].wait()
    keyval = nn(normed, w_keyval[...]).astype(BF16)
    keyval_ref[...] = keyval
    keys = keyval[:, :HD]
    values = keyval[:, HD:]
    row = lax.broadcasted_iota(jnp.int32, (slots, slots), 0)
    col = lax.broadcasted_iota(jnp.int32, (slots, slots), 1)
    across = jnp.where(row == col, starts_ref[...].reshape(1, slots), 0).astype(F32)
    starts = jnp.sum(across, axis=1, keepdims=True).astype(jnp.int32)
    allowed = (col >= starts) & (col <= row)
    for e in range(QPK):
        scores = nt(query[:, e * HD : (e + 1) * HD], keys) * (1.0 / math.sqrt(HD))
        scores = jnp.where(allowed, scores, -jnp.inf)
        expo = jnp.exp(scores - jnp.max(scores, axis=1, keepdims=True))
        probs = expo / jnp.sum(expo, axis=1, keepdims=True)
        probs_ref[e] = probs
        attn_ref[:, e * HD : (e + 1) * HD] = nn(probs.astype(BF16), values).astype(BF16)
    loads[2].wait()
    emit_blocks(core_ref[0], attn_ref, w_out, mine_ref, send_ref)


def total_kernel(got_ref, x_ref, out_hbm, sum_ref, sems):
    branch = got_ref[0].astype(F32)
    for n in range(1, got_ref.shape[0]):
        branch = branch + got_ref[n].astype(F32)
    sum_ref[...] = (x_ref[...].astype(F32) + branch).astype(BF16)
    stores = []
    for n in range(out_hbm.shape[0]):
        stores.append(pltpu.make_async_copy(sum_ref, out_hbm.at[n], sems.at[n]))
        stores[n].start()
    for store in stores:
        store.wait()


def backward_kernel(
    core_ref,
    count_ref,
    own_ref,
    other_ref,
    goal_ref,
    w_out_hbm,
    probs_hbm,
    keyval_hbm,
    query_hbm,
    w_query_hbm,
    w_keyval_hbm,
    mine_ref,
    send_ref,
    w_out,
    probs_ref,
    keyval_ref,
    query_ref,
    w_query,
    w_keyval,
    dyb_ref,
    grads_ref,
    sems,
):
    loads = [
        pltpu.make_async_copy(source, target, sems.at[n])
        for n, (source, target) in enumerate(
            (
                (w_out_hbm, w_out),
                (probs_hbm, probs_ref),
                (keyval_hbm, keyval_ref),
                (query_hbm, query_ref),
                (w_query_hbm, w_query),
                (w_keyval_hbm, w_keyval),
            )
        )
    ]
    for load in loads:
        load.start()
    core = core_ref[0]
    count = count_ref[0]
    slots, width = goal_ref.shape
    high, wide = own_ref.shape[1:]
    for c in range(2):
        for i in range(2):
            first = (2 * c + i) * high
            y, t = [], []
            for j in range(COLS):
                n = i * COLS + j
                y.append(jnp.where(core == c, own_ref[n].astype(F32), other_ref[n].astype(F32)))
                t.append(goal_ref[first : first + high, j * wide : (j + 1) * wide].astype(F32))
            place = lax.broadcasted_iota(jnp.int32, (high, 1), 0) + first
            t_scale, y_scale = direction(y, t, (place < count).astype(F32), width)
            for j in range(COLS):
                dy = t[j] * t_scale - y[j] * y_scale
                dyb_ref[first : first + high, j * wide : (j + 1) * wide] = dy.astype(BF16)
    loads[0].wait()
    d_attn = nt(dyb_ref[...], w_out[...]).astype(BF16)
    for load in loads[1:4]:
        load.wait()
    keys = keyval_ref[:, :HD]
    values = keyval_ref[:, HD:]
    d_keys = d_values = None
    for e in range(QPK):
        head = slice(e * HD, (e + 1) * HD)
        d_out = d_attn[:, head]
        probs = probs_ref[e]
        d_value = tn(probs.astype(BF16), d_out)
        dprob = nt(d_out, values)
        dscore = probs * (dprob - jnp.sum(dprob * probs, axis=1, keepdims=True))
        dscore = (dscore * (1.0 / math.sqrt(HD))).astype(BF16)
        grads_ref[:, head] = nn(dscore, keys).astype(BF16)
        d_key = tn(dscore, query_ref[:, head])
        d_keys = d_key if d_keys is None else d_keys + d_key
        d_values = d_value if d_values is None else d_values + d_value
    grads_ref[:, QPK * HD : (QPK + 1) * HD] = d_keys.astype(BF16)
    grads_ref[:, (QPK + 1) * HD :] = d_values.astype(BF16)
    half = slots // 2
    row = lax.broadcasted_iota(jnp.int32, (slots, slots), 0)
    col = lax.broadcasted_iota(jnp.int32, (slots, slots), 1)
    sent = (row >= half).astype(jnp.int32)
    place = row - half * sent
    parity = core + sent - 2 * core * sent
    late = (place >= 64).astype(jnp.int32)
    early_row = 20 * (place >> 3) + (place & 7)
    late_row = 20 * ((place - 64) >> 1) + 8 + (place & 1)
    source = early_row + late * (late_row - early_row) + 10 * parity
    pick = (col == source).astype(BF16)
    rows = nn(pick, grads_ref[...]).astype(BF16)
    for load in loads[4:]:
        load.wait()
    sub = lax.broadcasted_iota(jnp.int32, (8, HD), 0) >> 1
    for j in range(width // (4 * HD)):
        span = slice(j * 4 * HD, (j + 1) * 4 * HD)
        part = nt(rows[:, : QPK * HD], w_query[span, :]) + nt(rows[:, QPK * HD :], w_keyval[span, :])
        for h, ref in ((0, mine_ref), (1, send_ref)):
            base = h * half
            for k in range(4):
                lane = slice(k * HD, (k + 1) * HD)
                at = 8 * (4 * j + k)
                for n in range(8):
                    ref[n, at : at + 8, :] = part[base + 8 * n : base + 8 * n + 8, lane].astype(BF16)
            for g in range(2):
                low = base + 64 + 8 * g
                tiles = [part[low : low + 8, k * HD : (k + 1) * HD] for k in range(4)]
                for i in range(4):
                    tile = None
                    for k in range(4):
                        turned = pltpu.roll(tiles[k], (2 * k - 2 * i) % 8, 0) if k != i else tiles[k]
                        tile = turned if tile is None else jnp.where(sub == k, turned, tile)
                    at = 224 + 8 * j
                    ref[4 * g + i, at : at + 8, :] = tile.astype(BF16)


def final_kernel(got_ref, x_ref, dy_ref, gain_ref, out_ref, rows_ref):
    total = got_ref[0].astype(F32)
    for n in range(1, got_ref.shape[0]):
        total = total + got_ref[n].astype(F32)
    for t in range(28):
        lane = slice(t * HD, (t + 1) * HD)
        rows_ref[0:8, lane] = total[8 * t : 8 * t + 8]
        at = 224 + 2 * t
        rows_ref[8:10, lane] = total[at : at + 2]
    x = x_ref[...]
    inv = lax.rsqrt(jnp.mean(x * x, axis=1, keepdims=True) + epsilon)
    upper = rows_ref[0:10, :] * gain_ref[...].reshape(1, x.shape[1])
    dx = inv * upper - x * (inv * inv * inv) * jnp.mean(upper * x, axis=1, keepdims=True)
    out_ref[...] = (dy_ref[...] + dx).astype(BF16)


def from_behind(block, axis, distance):
    devices = range(lax.axis_size(axis))
    route = [(i - distance, i) for i in devices if i - distance in devices]
    return lax.ppermute(block, axis, route)


def swap(block):
    return lax.ppermute(block, "core", PAIR)


def call(kernel, outs, scratch, *args, far=0, place=VMEM):
    specs = [SMEM if a.shape == (1,) else VMEM for a in args]
    specs[len(args) - far :] = [HBM] * far
    return pl.pallas_call(
        kernel,
        out_shape=outs,
        in_specs=specs,
        out_specs=jax.tree.map(lambda _: place, outs),
        scratch_shapes=scratch,
    )(*args)


def spread(mine, send):
    out = shape(mine.shape, BF16)
    scratch = [pltpu.VMEM(out.shape, BF16), pltpu.SemaphoreType.DMA((8,))]
    chip = call(pair_kernel, out, scratch, mine, near(swap(send)), place=HBM)
    return lax.all_to_all(chip, "y", 0, 0)


def body(
    teacher_hidden,
    proj_weight,
    student_in,
    norm_gain,
    w_query,
    w_keyval,
    w_out,
    row_offsets,
    row_counts,
    doc_start,
):
    tokens_here = teacher_hidden.shape[0]
    quarter = tokens_here // 4
    slots, width = student_in.shape
    high, wide = slots // 4, width // COLS
    core = lax.axis_index("core")
    ypos = lax.axis_index("y")
    core_s = core.astype(jnp.int32).reshape(1)
    start = row_offsets - lax.axis_index("seq") * tokens_here + quarter
    blocks = shape((8, high, wide), BF16)
    parts = shape((8, quarter, wide), BF16)
    goal_mine, goal_send = call(
        goal_kernel,
        (parts, parts),
        [pltpu.VMEM(proj_weight.shape, BF16), pltpu.SemaphoreType.DMA((COLS,))],
        core_s,
        teacher_hidden,
        proj_weight,
        far=1,
    )
    goal_got = spread(goal_mine, goal_send)
    query, keyval, probs, mine, send = pl.pallas_call(
        forward_kernel,
        out_shape=(
            shape((slots, QPK * HD), BF16),
            shape((slots, 2 * HD), BF16),
            shape((QPK, slots, slots), F32),
            blocks,
            blocks,
        ),
        in_specs=[SMEM, VMEM, VMEM, VMEM, HBM, HBM, HBM],
        out_specs=(VMEM,) * 5,
        scratch_shapes=[
            pltpu.VMEM(w_query.shape, BF16),
            pltpu.VMEM(w_keyval.shape, BF16),
            pltpu.VMEM(w_out.shape, BF16),
            pltpu.VMEM((slots, QPK * HD), BF16),
            pltpu.SemaphoreType.DMA((3,)),
        ],
        name="forward",
    )(core_s, student_in, norm_gain, doc_start, w_query, w_keyval, w_out)
    branch_got = spread(mine, send)
    goal_own = jnp.sum(goal_got.astype(F32), axis=0).astype(BF16)
    goal_rows = lax.all_gather(goal_own, TP)
    earlier = goal_rows.reshape(2, COLS, 2, quarter, wide)[1, :, 1]
    earlier = from_behind(earlier, "seq", 1)
    goal = call(align_kernel, shape((slots, width), BF16), (), start, goal_rows, earlier)
    x_block = lax.dynamic_slice(
        student_in,
        (core * (slots // 2) + (ypos // COLS) * high, (ypos % COLS) * wide),
        (high, wide),
    )
    y_own = call(
        total_kernel,
        blocks,
        [pltpu.VMEM((high, wide), BF16), pltpu.SemaphoreType.DMA((8,))],
        near(branch_got),
        x_block,
        place=HBM,
    )
    y_half = lax.all_to_all(y_own, "y", 0, 0)
    y_other = swap(y_half)
    pieces = shape((8, slots // 16 * (width // HD), HD), BF16)
    saved = (w_out, probs, keyval, query, w_query, w_keyval)
    mine, send = call(
        backward_kernel,
        (pieces, pieces),
        [pltpu.VMEM(a.shape, a.dtype) for a in saved]
        + [
            pltpu.VMEM((slots, width), BF16),
            pltpu.VMEM((slots, (QPK + 2) * HD), BF16),
            pltpu.SemaphoreType.DMA((len(saved),)),
        ],
        core_s,
        row_counts,
        near(y_half),
        near(y_other),
        goal,
        *saved,
        far=len(saved),
    )
    got = spread(mine, send)
    own_rows = slots // 16
    first_row = ((ypos * 2 + core) * own_rows).astype(jnp.int32).reshape(1)
    rows = shape((own_rows, width), F32)
    student_out, dy_own, x_own = call(
        finish_kernel,
        (shape((slots, width), BF16), rows, rows),
        (),
        core_s,
        first_row,
        row_counts,
        y_half,
        y_other,
        goal,
        student_in,
    )
    grad_in = call(
        final_kernel,
        shape((own_rows, width), BF16),
        [pltpu.VMEM((16, width), F32)],
        near(got),
        x_own,
        dy_own,
        norm_gain,
    )
    return (student_out, grad_in)


def solution(mesh):
    seqs, tps = mesh.devices.shape
    split = Mesh(mesh.devices.reshape(seqs, tps // 2, 2), ("seq",) + TP)
    in_specs = (
        P("seq", TP),
        P(TP, None),
        P("seq", None),
        P(),
        P(None, TP),
        P(None, TP),
        P(TP, None),
        P("seq"),
        P("seq"),
        P("seq"),
    )
    out_specs = (P("seq", None), P(("seq",) + TP, None))
    return jax.shard_map(body, mesh=split, in_specs=in_specs, out_specs=out_specs, check_vma=False)
```

```python
import math

import jax
import jax.numpy as jnp
from jax import lax
from jax.experimental import pallas as pl
from jax.experimental.pallas import tpu as pltpu
from jax.sharding import Mesh
from jax.sharding import PartitionSpec as P

HD = 128
QPK = 2
PAIR = [(0, 1), (1, 0)]
COLS = 4
TP = ("y", "core")

epsilon = 1e-06

VMEM = pl.BlockSpec(memory_space=pltpu.VMEM)
SMEM = pl.BlockSpec(memory_space=pltpu.SMEM)
HBM = pl.BlockSpec(memory_space=pltpu.HBM)
F32 = jnp.float32
BF16 = jnp.bfloat16


def near(array):
    return pltpu.with_memory_space_constraint(array, pltpu.VMEM)


def shape(dims, dtype):
    return jax.ShapeDtypeStruct(dims, dtype)


def nt(a, b):
    return lax.dot_general(a, b, (((1,), (1,)), ((), ())), preferred_element_type=F32)


def tn(a, b):
    return lax.dot_general(a, b, (((0,), (0,)), ((), ())), preferred_element_type=F32)


def nn(a, b):
    return jnp.dot(a, b, preferred_element_type=F32)


def emit_blocks(core, lhs_ref, weight_ref, mine_ref, send_ref, loads=()):
    half = lhs_ref.shape[0] // 2
    high, wide = mine_ref.shape[1:]
    first = lhs_ref[pl.ds(pl.multiple_of(core * half, 16), half), :]
    second = lhs_ref[pl.ds(pl.multiple_of((1 - core) * half, 16), half), :]
    lhs = jnp.concatenate([first, second], axis=0)
    for j in range(COLS):
        if loads:
            loads[j].wait()
        out = nn(lhs, weight_ref[:, j * wide : (j + 1) * wide])
        for i in range(2):
            mine_ref[i * COLS + j] = out[i * high : (i + 1) * high].astype(BF16)
            send_ref[i * COLS + j] = out[half + i * high : half + (i + 1) * high].astype(BF16)


def goal_kernel(core_ref, rows_ref, weight_hbm, mine_ref, send_ref, weight_ref, sems):
    wide = mine_ref.shape[2]
    loads = []
    for j in range(COLS):
        span = slice(j * wide, (j + 1) * wide)
        load = pltpu.make_async_copy(weight_hbm.at[:, span], weight_ref.at[:, span], sems.at[j])
        load.start()
        loads.append(load)
    emit_blocks(core_ref[0], rows_ref, weight_ref, mine_ref, send_ref, loads)


def pair_kernel(mine_ref, other_ref, out_hbm, sum_ref, sems):
    stores = []
    for n in range(out_hbm.shape[0]):
        sum_ref[n] = (mine_ref[n].astype(F32) + other_ref[n].astype(F32)).astype(BF16)
        stores.append(pltpu.make_async_copy(sum_ref.at[n], out_hbm.at[n], sems.at[n]))
        stores[n].start()
    for store in stores:
        store.wait()


def first_kernel(y_ref, mine_ref, other_ref, up_ref, down_ref, keep_ref):
    for ref, away in ((up_ref, (1, 4, -2)), (down_ref, (-1, 2)), (keep_ref, (0, 3, -3))):
        for k, r in enumerate(away):
            n = (y_ref[0] + (r + 8)) & 7
            ref[k] = (mine_ref[n].astype(F32) + other_ref[n].astype(F32)).astype(BF16)


def second_kernel(keep_ref, below_ref, above_ref, own_ref, plus_ref, minus_ref):
    def at(ref, k):
        return ref[k].astype(F32)

    own_ref[...] = at(keep_ref, 0) + at(below_ref, 0) + at(above_ref, 0)
    plus = at(keep_ref, 1) + at(below_ref, 1) + at(above_ref, 1)
    plus_ref[...] = plus.astype(BF16)
    minus_ref[...] = (at(keep_ref, 2) + at(below_ref, 2)).astype(BF16)


def align_kernel(start_ref, own_ref, earlier_ref, out_ref):
    slots = out_ref.shape[0]
    wide = own_ref.shape[2]
    row = lax.broadcasted_iota(jnp.int32, (slots, slots), 0)
    col = lax.broadcasted_iota(jnp.int32, (slots, slots), 1)
    pick = (col == row + start_ref[0]).astype(BF16)
    for j in range(COLS):
        bands = [earlier_ref[j]]
        for c in range(2):
            for i in range(2):
                bands.append(own_ref[2 * (i * COLS + j) + c])
        rows = jnp.concatenate(bands, axis=0)
        out_ref[:, j * wide : (j + 1) * wide] = nn(pick, rows).astype(BF16)


def direction(y, t, live, width):
    asum = sum(jnp.sum(a * a, axis=1, keepdims=True) for a in y) + epsilon
    bsum = sum(jnp.sum(a * a, axis=1, keepdims=True) for a in t) + epsilon
    dots = sum(jnp.sum(a * b, axis=1, keepdims=True) for a, b in zip(y, t))
    both = lax.rsqrt(asum * bsum)
    factor = -math.sqrt(width) * live
    return factor * both, factor * (dots * both) / asum


def finish_kernel(
    core_ref, first_ref, count_ref, own_ref, other_ref, goal_ref, x_ref, student_ref, dy_ref, x_own_ref
):
    core = core_ref[0]
    slots, width = student_ref.shape
    high, wide = own_ref.shape[1:]
    for c in range(2):
        for i in range(2):
            first = (2 * c + i) * high
            for j in range(COLS):
                n = i * COLS + j
                block = jnp.where(core == c, own_ref[n].astype(F32), other_ref[n].astype(F32))
                student_ref[first : first + high, j * wide : (j + 1) * wide] = block.astype(BF16)
    own_rows = dy_ref.shape[0]
    row = lax.broadcasted_iota(jnp.int32, (16, slots), 0) + first_ref[0]
    col = lax.broadcasted_iota(jnp.int32, (16, slots), 1)
    pick = (col == row).astype(BF16)
    y = nn(pick, student_ref[...])
    t = nn(pick, goal_ref[...])
    x_own_ref[...] = nn(pick, x_ref[...])[:own_rows]
    place = lax.broadcasted_iota(jnp.int32, (16, 1), 0) + first_ref[0]
    t_scale, y_scale = direction([y], [t], (place < count_ref[0]).astype(F32), width)
    dy_ref[...] = (t * t_scale - y * y_scale)[:own_rows]


def forward_kernel(
    core_ref,
    x_ref,
    gain_ref,
    starts_ref,
    w_query_hbm,
    w_keyval_hbm,
    w_out_hbm,
    query_ref,
    keyval_ref,
    probs_ref,
    mine_ref,
    send_ref,
    w_query,
    w_keyval,
    w_out,
    attn_ref,
    sems,
):
    loads = [
        pltpu.make_async_copy(source, target, sems.at[n])
        for n, (source, target) in enumerate(
            ((w_query_hbm, w_query), (w_keyval_hbm, w_keyval), (w_out_hbm, w_out))
        )
    ]
    for load in loads:
        load.start()
    slots = x_ref.shape[0]
    xf = x_ref[...].astype(F32)
    inv = lax.rsqrt(jnp.mean(xf * xf, axis=1, keepdims=True) + epsilon)
    normed = (xf * inv * gain_ref[...].reshape(1, xf.shape[1])).astype(BF16)
    loads[0].wait()
    query = nn(normed, w_query[...]).astype(BF16)
    query_ref[...] = query
    loads[1].wait()
    keyval = nn(normed, w_keyval[...]).astype(BF16)
    keyval_ref[...] = keyval
    keys = keyval[:, :HD]
    values = keyval[:, HD:]
    row = lax.broadcasted_iota(jnp.int32, (slots, slots), 0)
    col = lax.broadcasted_iota(jnp.int32, (slots, slots), 1)
    across = jnp.where(row == col, starts_ref[...].reshape(1, slots), 0).astype(F32)
    starts = jnp.sum(across, axis=1, keepdims=True).astype(jnp.int32)
    allowed = (col >= starts) & (col <= row)
    for e in range(QPK):
        scores = nt(query[:, e * HD : (e + 1) * HD], keys) * (1.0 / math.sqrt(HD))
        scores = jnp.where(allowed, scores, -jnp.inf)
        expo = jnp.exp(scores - jnp.max(scores, axis=1, keepdims=True))
        probs = expo / jnp.sum(expo, axis=1, keepdims=True)
        probs_ref[e] = probs
        attn_ref[:, e * HD : (e + 1) * HD] = nn(probs.astype(BF16), values).astype(BF16)
    loads[2].wait()
    emit_blocks(core_ref[0], attn_ref, w_out, mine_ref, send_ref)


def total_kernel(got_ref, x_ref, out_hbm, sum_ref, sems):
    branch = got_ref[0].astype(F32)
    for n in range(1, got_ref.shape[0]):
        branch = branch + got_ref[n].astype(F32)
    sum_ref[...] = (x_ref[...].astype(F32) + branch).astype(BF16)
    stores = []
    for n in range(out_hbm.shape[0]):
        stores.append(pltpu.make_async_copy(sum_ref, out_hbm.at[n], sems.at[n]))
        stores[n].start()
    for store in stores:
        store.wait()


def backward_kernel(
    core_ref,
    count_ref,
    own_ref,
    other_ref,
    goal_ref,
    w_out_hbm,
    probs_hbm,
    keyval_hbm,
    query_hbm,
    w_query_hbm,
    w_keyval_hbm,
    mine_ref,
    send_ref,
    w_out,
    probs_ref,
    keyval_ref,
    query_ref,
    w_query,
    w_keyval,
    dyb_ref,
    grads_ref,
    sems,
):
    loads = [
        pltpu.make_async_copy(source, target, sems.at[n])
        for n, (source, target) in enumerate(
            (
                (w_out_hbm, w_out),
                (probs_hbm, probs_ref),
                (keyval_hbm, keyval_ref),
                (query_hbm, query_ref),
                (w_query_hbm, w_query),
                (w_keyval_hbm, w_keyval),
            )
        )
    ]
    for load in loads:
        load.start()
    core = core_ref[0]
    count = count_ref[0]
    slots, width = goal_ref.shape
    high, wide = own_ref.shape[1:]
    for c in range(2):
        for i in range(2):
            first = (2 * c + i) * high
            y, t = [], []
            for j in range(COLS):
                n = i * COLS + j
                y.append(jnp.where(core == c, own_ref[n].astype(F32), other_ref[n].astype(F32)))
                t.append(goal_ref[first : first + high, j * wide : (j + 1) * wide].astype(F32))
            place = lax.broadcasted_iota(jnp.int32, (high, 1), 0) + first
            t_scale, y_scale = direction(y, t, (place < count).astype(F32), width)
            for j in range(COLS):
                dy = t[j] * t_scale - y[j] * y_scale
                dyb_ref[first : first + high, j * wide : (j + 1) * wide] = dy.astype(BF16)
    loads[0].wait()
    d_attn = nt(dyb_ref[...], w_out[...]).astype(BF16)
    for load in loads[1:4]:
        load.wait()
    keys = keyval_ref[:, :HD]
    values = keyval_ref[:, HD:]
    d_keys = d_values = None
    for e in range(QPK):
        head = slice(e * HD, (e + 1) * HD)
        d_out = d_attn[:, head]
        probs = probs_ref[e]
        d_value = tn(probs.astype(BF16), d_out)
        dprob = nt(d_out, values)
        dscore = probs * (dprob - jnp.sum(dprob * probs, axis=1, keepdims=True))
        dscore = (dscore * (1.0 / math.sqrt(HD))).astype(BF16)
        grads_ref[:, head] = nn(dscore, keys).astype(BF16)
        d_key = tn(dscore, query_ref[:, head])
        d_keys = d_key if d_keys is None else d_keys + d_key
        d_values = d_value if d_values is None else d_values + d_value
    grads_ref[:, QPK * HD : (QPK + 1) * HD] = d_keys.astype(BF16)
    grads_ref[:, (QPK + 1) * HD :] = d_values.astype(BF16)
    half = slots // 2
    row = lax.broadcasted_iota(jnp.int32, (slots, slots), 0)
    col = lax.broadcasted_iota(jnp.int32, (slots, slots), 1)
    sent = (row >= half).astype(jnp.int32)
    place = row - half * sent
    parity = core + sent - 2 * core * sent
    late = (place >= 64).astype(jnp.int32)
    early_row = 20 * (place >> 3) + (place & 7)
    late_row = 20 * ((place - 64) >> 1) + 8 + (place & 1)
    source = early_row + late * (late_row - early_row) + 10 * parity
    pick = (col == source).astype(BF16)
    rows = nn(pick, grads_ref[...]).astype(BF16)
    for load in loads[4:]:
        load.wait()
    sub = lax.broadcasted_iota(jnp.int32, (8, HD), 0) >> 1
    for j in range(width // (4 * HD)):
        span = slice(j * 4 * HD, (j + 1) * 4 * HD)
        part = nt(rows[:, : QPK * HD], w_query[span, :]) + nt(rows[:, QPK * HD :], w_keyval[span, :])
        for h, ref in ((0, mine_ref), (1, send_ref)):
            base = h * half
            for k in range(4):
                lane = slice(k * HD, (k + 1) * HD)
                at = 8 * (4 * j + k)
                for n in range(8):
                    ref[n, at : at + 8, :] = part[base + 8 * n : base + 8 * n + 8, lane].astype(BF16)
            for g in range(2):
                low = base + 64 + 8 * g
                tiles = [part[low : low + 8, k * HD : (k + 1) * HD] for k in range(4)]
                for i in range(4):
                    tile = None
                    for k in range(4):
                        turned = pltpu.roll(tiles[k], (2 * k - 2 * i) % 8, 0) if k != i else tiles[k]
                        tile = turned if tile is None else jnp.where(sub == k, turned, tile)
                    at = 224 + 8 * j
                    ref[4 * g + i, at : at + 8, :] = tile.astype(BF16)


def final_kernel(got_ref, x_ref, dy_ref, gain_ref, out_ref, rows_ref):
    total = got_ref[0].astype(F32)
    for n in range(1, got_ref.shape[0]):
        total = total + got_ref[n].astype(F32)
    for t in range(28):
        lane = slice(t * HD, (t + 1) * HD)
        rows_ref[0:8, lane] = total[8 * t : 8 * t + 8]
        at = 224 + 2 * t
        rows_ref[8:10, lane] = total[at : at + 2]
    x = x_ref[...]
    inv = lax.rsqrt(jnp.mean(x * x, axis=1, keepdims=True) + epsilon)
    upper = rows_ref[0:10, :] * gain_ref[...].reshape(1, x.shape[1])
    dx = inv * upper - x * (inv * inv * inv) * jnp.mean(upper * x, axis=1, keepdims=True)
    out_ref[...] = (dy_ref[...] + dx).astype(BF16)


def from_behind(block, axis, distance):
    devices = range(lax.axis_size(axis))
    route = [(i - distance, i) for i in devices if i - distance in devices]
    return lax.ppermute(block, axis, route)


def swap(block):
    return lax.ppermute(block, "core", PAIR)


def turn(block, distance):
    size = lax.axis_size("y")
    return lax.ppermute(block, "y", [(i, (i + distance) % size) for i in range(size)])


def call(kernel, outs, scratch, *args, far=0, place=VMEM):
    specs = [SMEM if a.shape == (1,) else VMEM for a in args]
    specs[len(args) - far :] = [HBM] * far
    return pl.pallas_call(
        kernel,
        out_shape=outs,
        in_specs=specs,
        out_specs=jax.tree.map(lambda _: place, outs),
        scratch_shapes=scratch,
    )(*args)


def spread(mine, send):
    out = shape(mine.shape, BF16)
    scratch = [pltpu.VMEM(out.shape, BF16), pltpu.SemaphoreType.DMA((8,))]
    chip = call(pair_kernel, out, scratch, mine, near(swap(send)), place=HBM)
    return lax.all_to_all(chip, "y", 0, 0)


def body(
    teacher_hidden,
    proj_weight,
    student_in,
    norm_gain,
    w_query,
    w_keyval,
    w_out,
    row_offsets,
    row_counts,
    doc_start,
):
    tokens_here = teacher_hidden.shape[0]
    quarter = tokens_here // 4
    slots, width = student_in.shape
    high, wide = slots // 4, width // COLS
    core = lax.axis_index("core")
    ypos = lax.axis_index("y")
    core_s = core.astype(jnp.int32).reshape(1)
    start = row_offsets - lax.axis_index("seq") * tokens_here + quarter
    blocks = shape((8, high, wide), BF16)
    parts = shape((8, quarter, wide), BF16)
    goal_mine, goal_send = call(
        goal_kernel,
        (parts, parts),
        [pltpu.VMEM(proj_weight.shape, BF16), pltpu.SemaphoreType.DMA((COLS,))],
        core_s,
        teacher_hidden,
        proj_weight,
        far=1,
    )
    some = [shape((n, quarter, wide), BF16) for n in (3, 2, 3)]
    ypos_s = ypos.astype(jnp.int32).reshape(1)
    up, down, keep = call(first_kernel, tuple(some), (), ypos_s, goal_mine, near(swap(goal_send)))
    one = (quarter, wide)
    own, plus, minus = call(
        second_kernel,
        (shape(one, F32), shape(one, BF16), shape(one, BF16)),
        (),
        keep,
        near(turn(up, 1)),
        near(turn(down, -1)),
    )
    plus = turn(plus, 3)
    minus = turn(minus, -3)
    goal_own = (own + plus.astype(F32) + minus.astype(F32)).astype(BF16)
    query, keyval, probs, mine, send = pl.pallas_call(
        forward_kernel,
        out_shape=(
            shape((slots, QPK * HD), BF16),
            shape((slots, 2 * HD), BF16),
            shape((QPK, slots, slots), F32),
            blocks,
            blocks,
        ),
        in_specs=[SMEM, VMEM, VMEM, VMEM, HBM, HBM, HBM],
        out_specs=(VMEM,) * 5,
        scratch_shapes=[
            pltpu.VMEM(w_query.shape, BF16),
            pltpu.VMEM(w_keyval.shape, BF16),
            pltpu.VMEM(w_out.shape, BF16),
            pltpu.VMEM((slots, QPK * HD), BF16),
            pltpu.SemaphoreType.DMA((3,)),
        ],
        name="forward",
    )(core_s, student_in, norm_gain, doc_start, w_query, w_keyval, w_out)
    branch_got = spread(mine, send)
    goal_rows = lax.all_gather(goal_own, TP)
    earlier = goal_rows.reshape(2, COLS, 2, quarter, wide)[1, :, 1]
    earlier = from_behind(earlier, "seq", 1)
    goal = call(align_kernel, shape((slots, width), BF16), (), start, goal_rows, earlier)
    x_block = lax.dynamic_slice(
        student_in,
        (core * (slots // 2) + (ypos // COLS) * high, (ypos % COLS) * wide),
        (high, wide),
    )
    y_own = call(
        total_kernel,
        blocks,
        [pltpu.VMEM((high, wide), BF16), pltpu.SemaphoreType.DMA((8,))],
        near(branch_got),
        x_block,
        place=HBM,
    )
    y_half = lax.all_to_all(y_own, "y", 0, 0)
    y_other = swap(y_half)
    pieces = shape((8, slots // 16 * (width // HD), HD), BF16)
    saved = (w_out, probs, keyval, query, w_query, w_keyval)
    mine, send = call(
        backward_kernel,
        (pieces, pieces),
        [pltpu.VMEM(a.shape, a.dtype) for a in saved]
        + [
            pltpu.VMEM((slots, width), BF16),
            pltpu.VMEM((slots, (QPK + 2) * HD), BF16),
            pltpu.SemaphoreType.DMA((len(saved),)),
        ],
        core_s,
        row_counts,
        near(y_half),
        near(y_other),
        goal,
        *saved,
        far=len(saved),
    )
    got = spread(mine, send)
    own_rows = slots // 16
    first_row = ((ypos * 2 + core) * own_rows).astype(jnp.int32).reshape(1)
    rows = shape((own_rows, width), F32)
    student_out, dy_own, x_own = call(
        finish_kernel,
        (shape((slots, width), BF16), rows, rows),
        (),
        core_s,
        first_row,
        row_counts,
        y_half,
        y_other,
        goal,
        student_in,
    )
    grad_in = call(
        final_kernel,
        shape((own_rows, width), BF16),
        [pltpu.VMEM((16, width), F32)],
        near(got),
        x_own,
        dy_own,
        norm_gain,
    )
    return (student_out, grad_in)


def solution(mesh):
    seqs, tps = mesh.devices.shape
    split = Mesh(mesh.devices.reshape(seqs, tps // 2, 2), ("seq",) + TP)
    in_specs = (
        P("seq", TP),
        P(TP, None),
        P("seq", None),
        P(),
        P(None, TP),
        P(None, TP),
        P(TP, None),
        P("seq"),
        P("seq"),
        P("seq"),
    )
    out_specs = (P("seq", None), P(("seq",) + TP, None))
    return jax.shard_map(body, mesh=split, in_specs=in_specs, out_specs=out_specs, check_vma=False)
```

```python
import math

import jax
import jax.numpy as jnp
from jax import lax
from jax.experimental import pallas as pl
from jax.experimental.pallas import tpu as pltpu
from jax.sharding import Mesh
from jax.sharding import PartitionSpec as P

HD = 128
QPK = 2
PAIR = [(0, 1), (1, 0)]
COLS = 4
TP = ("y", "core")

epsilon = 1e-06

VMEM = pl.BlockSpec(memory_space=pltpu.VMEM)
SMEM = pl.BlockSpec(memory_space=pltpu.SMEM)
HBM = pl.BlockSpec(memory_space=pltpu.HBM)
F32 = jnp.float32
BF16 = jnp.bfloat16


def near(array):
    return pltpu.with_memory_space_constraint(array, pltpu.VMEM)


def shape(dims, dtype):
    return jax.ShapeDtypeStruct(dims, dtype)


def nt(a, b):
    return lax.dot_general(a, b, (((1,), (1,)), ((), ())), preferred_element_type=F32)


def tn(a, b):
    return lax.dot_general(a, b, (((0,), (0,)), ((), ())), preferred_element_type=F32)


def nn(a, b):
    return jnp.dot(a, b, preferred_element_type=F32)


def emit_blocks(core, lhs_ref, weight_ref, mine_ref, send_ref, loads=()):
    half = lhs_ref.shape[0] // 2
    high, wide = mine_ref.shape[1:]
    first = lhs_ref[pl.ds(pl.multiple_of(core * half, 16), half), :]
    second = lhs_ref[pl.ds(pl.multiple_of((1 - core) * half, 16), half), :]
    lhs = jnp.concatenate([first, second], axis=0)
    for j in range(COLS):
        if loads:
            loads[j].wait()
        out = nn(lhs, weight_ref[:, j * wide : (j + 1) * wide])
        for i in range(2):
            mine_ref[i * COLS + j] = out[i * high : (i + 1) * high].astype(BF16)
            send_ref[i * COLS + j] = out[half + i * high : half + (i + 1) * high].astype(BF16)


def goal_kernel(core_ref, rows_ref, weight_hbm, mine_ref, send_ref, weight_ref, sems):
    wide = mine_ref.shape[2]
    loads = []
    for j in range(COLS):
        span = slice(j * wide, (j + 1) * wide)
        load = pltpu.make_async_copy(weight_hbm.at[:, span], weight_ref.at[:, span], sems.at[j])
        load.start()
        loads.append(load)
    emit_blocks(core_ref[0], rows_ref, weight_ref, mine_ref, send_ref, loads)


def pair_kernel(mine_ref, other_ref, out_hbm, sum_ref, sems):
    stores = []
    for n in range(out_hbm.shape[0]):
        sum_ref[n] = (mine_ref[n].astype(F32) + other_ref[n].astype(F32)).astype(BF16)
        stores.append(pltpu.make_async_copy(sum_ref.at[n], out_hbm.at[n], sems.at[n]))
        stores[n].start()
    for store in stores:
        store.wait()


def collect_kernel(y_ref, own_ref, far_ref, below_ref, above_ref, out_ref):
    own, low, high = 0, -3, 3

    def put(r, block):
        out_ref[(y_ref[0] + (r + 8)) & 7] = block

    put(own, own_ref[0])
    put(low, far_ref[0])
    put(high, far_ref[1])
    for k, r in enumerate((own, low, high)):
        put(r - 1, below_ref[k])
    for k, r in enumerate((own, low)):
        put(r + 1, above_ref[k])


def align_kernel(core_ref, start_ref, half_ref, other_ref, earlier_ref, out_ref):
    slots = out_ref.shape[0]
    wide = half_ref.shape[2]
    row = lax.broadcasted_iota(jnp.int32, (slots, slots), 0)
    col = lax.broadcasted_iota(jnp.int32, (slots, slots), 1)
    pick = (col == row + start_ref[0]).astype(BF16)
    for j in range(COLS):
        bands = [earlier_ref[j].astype(F32)]
        for c in range(2):
            for i in range(2):
                n = i * COLS + j
                bands.append(
                    jnp.where(core_ref[0] == c, half_ref[n].astype(F32), other_ref[n].astype(F32))
                )
        rows = jnp.concatenate(bands, axis=0).astype(BF16)
        out_ref[:, j * wide : (j + 1) * wide] = nn(pick, rows).astype(BF16)


def direction(y, t, live, width):
    asum = sum(jnp.sum(a * a, axis=1, keepdims=True) for a in y) + epsilon
    bsum = sum(jnp.sum(a * a, axis=1, keepdims=True) for a in t) + epsilon
    dots = sum(jnp.sum(a * b, axis=1, keepdims=True) for a, b in zip(y, t))
    both = lax.rsqrt(asum * bsum)
    factor = -math.sqrt(width) * live
    return factor * both, factor * (dots * both) / asum


def finish_kernel(
    core_ref, first_ref, count_ref, own_ref, other_ref, goal_ref, x_ref, student_ref, dy_ref, x_own_ref
):
    core = core_ref[0]
    slots, width = student_ref.shape
    high, wide = own_ref.shape[1:]
    for c in range(2):
        for i in range(2):
            first = (2 * c + i) * high
            for j in range(COLS):
                n = i * COLS + j
                block = jnp.where(core == c, own_ref[n].astype(F32), other_ref[n].astype(F32))
                student_ref[first : first + high, j * wide : (j + 1) * wide] = block.astype(BF16)
    own_rows = dy_ref.shape[0]
    row = lax.broadcasted_iota(jnp.int32, (16, slots), 0) + first_ref[0]
    col = lax.broadcasted_iota(jnp.int32, (16, slots), 1)
    pick = (col == row).astype(BF16)
    y = nn(pick, student_ref[...])
    t = nn(pick, goal_ref[...])
    x_own_ref[...] = nn(pick, x_ref[...])[:own_rows]
    place = lax.broadcasted_iota(jnp.int32, (16, 1), 0) + first_ref[0]
    t_scale, y_scale = direction([y], [t], (place < count_ref[0]).astype(F32), width)
    dy_ref[...] = (t * t_scale - y * y_scale)[:own_rows]


def forward_kernel(
    core_ref,
    x_ref,
    gain_ref,
    starts_ref,
    w_query_hbm,
    w_keyval_hbm,
    w_out_hbm,
    query_ref,
    keyval_ref,
    probs_ref,
    mine_ref,
    send_ref,
    w_query,
    w_keyval,
    w_out,
    attn_ref,
    sems,
):
    loads = [
        pltpu.make_async_copy(source, target, sems.at[n])
        for n, (source, target) in enumerate(
            ((w_query_hbm, w_query), (w_keyval_hbm, w_keyval), (w_out_hbm, w_out))
        )
    ]
    for load in loads:
        load.start()
    slots = x_ref.shape[0]
    xf = x_ref[...].astype(F32)
    inv = lax.rsqrt(jnp.mean(xf * xf, axis=1, keepdims=True) + epsilon)
    normed = (xf * inv * gain_ref[...].reshape(1, xf.shape[1])).astype(BF16)
    loads[0].wait()
    query = nn(normed, w_query[...]).astype(BF16)
    query_ref[...] = query
    loads[1].wait()
    keyval = nn(normed, w_keyval[...]).astype(BF16)
    keyval_ref[...] = keyval
    keys = keyval[:, :HD]
    values = keyval[:, HD:]
    row = lax.broadcasted_iota(jnp.int32, (slots, slots), 0)
    col = lax.broadcasted_iota(jnp.int32, (slots, slots), 1)
    across = jnp.where(row == col, starts_ref[...].reshape(1, slots), 0).astype(F32)
    starts = jnp.sum(across, axis=1, keepdims=True).astype(jnp.int32)
    allowed = (col >= starts) & (col <= row)
    for e in range(QPK):
        scores = nt(query[:, e * HD : (e + 1) * HD], keys) * (1.0 / math.sqrt(HD))
        scores = jnp.where(allowed, scores, -jnp.inf)
        expo = jnp.exp(scores - jnp.max(scores, axis=1, keepdims=True))
        probs = expo / jnp.sum(expo, axis=1, keepdims=True)
        probs_ref[e] = probs
        attn_ref[:, e * HD : (e + 1) * HD] = nn(probs.astype(BF16), values).astype(BF16)
    loads[2].wait()
    emit_blocks(core_ref[0], attn_ref, w_out, mine_ref, send_ref)


def total_kernel(got_ref, x_ref, out_hbm, sum_ref, sems):
    branch = got_ref[0].astype(F32)
    for n in range(1, got_ref.shape[0]):
        branch = branch + got_ref[n].astype(F32)
    sum_ref[...] = (x_ref[...].astype(F32) + branch).astype(BF16)
    stores = []
    for n in range(out_hbm.shape[0]):
        stores.append(pltpu.make_async_copy(sum_ref, out_hbm.at[n], sems.at[n]))
        stores[n].start()
    for store in stores:
        store.wait()


def backward_kernel(
    core_ref,
    count_ref,
    own_ref,
    other_ref,
    goal_ref,
    w_out_hbm,
    probs_hbm,
    keyval_hbm,
    query_hbm,
    w_query_hbm,
    w_keyval_hbm,
    mine_ref,
    send_ref,
    w_out,
    probs_ref,
    keyval_ref,
    query_ref,
    w_query,
    w_keyval,
    dyb_ref,
    grads_ref,
    sems,
):
    loads = [
        pltpu.make_async_copy(source, target, sems.at[n])
        for n, (source, target) in enumerate(
            (
                (w_out_hbm, w_out),
                (probs_hbm, probs_ref),
                (keyval_hbm, keyval_ref),
                (query_hbm, query_ref),
                (w_query_hbm, w_query),
                (w_keyval_hbm, w_keyval),
            )
        )
    ]
    for load in loads:
        load.start()
    core = core_ref[0]
    count = count_ref[0]
    slots, width = goal_ref.shape
    high, wide = own_ref.shape[1:]
    for c in range(2):
        for i in range(2):
            first = (2 * c + i) * high
            y, t = [], []
            for j in range(COLS):
                n = i * COLS + j
                y.append(jnp.where(core == c, own_ref[n].astype(F32), other_ref[n].astype(F32)))
                t.append(goal_ref[first : first + high, j * wide : (j + 1) * wide].astype(F32))
            place = lax.broadcasted_iota(jnp.int32, (high, 1), 0) + first
            t_scale, y_scale = direction(y, t, (place < count).astype(F32), width)
            for j in range(COLS):
                dy = t[j] * t_scale - y[j] * y_scale
                dyb_ref[first : first + high, j * wide : (j + 1) * wide] = dy.astype(BF16)
    loads[0].wait()
    d_attn = nt(dyb_ref[...], w_out[...]).astype(BF16)
    for load in loads[1:4]:
        load.wait()
    keys = keyval_ref[:, :HD]
    values = keyval_ref[:, HD:]
    d_keys = d_values = None
    for e in range(QPK):
        head = slice(e * HD, (e + 1) * HD)
        d_out = d_attn[:, head]
        probs = probs_ref[e]
        d_value = tn(probs.astype(BF16), d_out)
        dprob = nt(d_out, values)
        dscore = probs * (dprob - jnp.sum(dprob * probs, axis=1, keepdims=True))
        dscore = (dscore * (1.0 / math.sqrt(HD))).astype(BF16)
        grads_ref[:, head] = nn(dscore, keys).astype(BF16)
        d_key = tn(dscore, query_ref[:, head])
        d_keys = d_key if d_keys is None else d_keys + d_key
        d_values = d_value if d_values is None else d_values + d_value
    grads_ref[:, QPK * HD : (QPK + 1) * HD] = d_keys.astype(BF16)
    grads_ref[:, (QPK + 1) * HD :] = d_values.astype(BF16)
    half = slots // 2
    row = lax.broadcasted_iota(jnp.int32, (slots, slots), 0)
    col = lax.broadcasted_iota(jnp.int32, (slots, slots), 1)
    sent = (row >= half).astype(jnp.int32)
    place = row - half * sent
    parity = core + sent - 2 * core * sent
    late = (place >= 64).astype(jnp.int32)
    early_row = 20 * (place >> 3) + (place & 7)
    late_row = 20 * ((place - 64) >> 1) + 8 + (place & 1)
    source = early_row + late * (late_row - early_row) + 10 * parity
    pick = (col == source).astype(BF16)
    rows = nn(pick, grads_ref[...]).astype(BF16)
    for load in loads[4:]:
        load.wait()
    sub = lax.broadcasted_iota(jnp.int32, (8, HD), 0) >> 1
    for j in range(width // (4 * HD)):
        span = slice(j * 4 * HD, (j + 1) * 4 * HD)
        part = nt(rows[:, : QPK * HD], w_query[span, :]) + nt(rows[:, QPK * HD :], w_keyval[span, :])
        for h, ref in ((0, mine_ref), (1, send_ref)):
            base = h * half
            for k in range(4):
                lane = slice(k * HD, (k + 1) * HD)
                at = 8 * (4 * j + k)
                for n in range(8):
                    ref[n, at : at + 8, :] = part[base + 8 * n : base + 8 * n + 8, lane].astype(BF16)
            for g in range(2):
                low = base + 64 + 8 * g
                tiles = [part[low : low + 8, k * HD : (k + 1) * HD] for k in range(4)]
                for i in range(4):
                    tile = None
                    for k in range(4):
                        turned = pltpu.roll(tiles[k], (2 * k - 2 * i) % 8, 0) if k != i else tiles[k]
                        tile = turned if tile is None else jnp.where(sub == k, turned, tile)
                    at = 224 + 8 * j
                    ref[4 * g + i, at : at + 8, :] = tile.astype(BF16)


def final_kernel(got_ref, x_ref, dy_ref, gain_ref, out_ref, rows_ref):
    total = got_ref[0].astype(F32)
    for n in range(1, got_ref.shape[0]):
        total = total + got_ref[n].astype(F32)
    for t in range(28):
        lane = slice(t * HD, (t + 1) * HD)
        rows_ref[0:8, lane] = total[8 * t : 8 * t + 8]
        at = 224 + 2 * t
        rows_ref[8:10, lane] = total[at : at + 2]
    x = x_ref[...]
    inv = lax.rsqrt(jnp.mean(x * x, axis=1, keepdims=True) + epsilon)
    upper = rows_ref[0:10, :] * gain_ref[...].reshape(1, x.shape[1])
    dx = inv * upper - x * (inv * inv * inv) * jnp.mean(upper * x, axis=1, keepdims=True)
    out_ref[...] = (dy_ref[...] + dx).astype(BF16)


def from_behind(block, axis, distance):
    devices = range(lax.axis_size(axis))
    route = [(i - distance, i) for i in devices if i - distance in devices]
    return lax.ppermute(block, axis, route)


def swap(block):
    return lax.ppermute(block, "core", PAIR)


def turn(block, distance):
    size = lax.axis_size("y")
    return lax.ppermute(block, "y", [(i, (i + distance) % size) for i in range(size)])


def call(kernel, outs, scratch, *args, far=0, place=VMEM):
    specs = [SMEM if a.shape == (1,) else VMEM for a in args]
    specs[len(args) - far :] = [HBM] * far
    return pl.pallas_call(
        kernel,
        out_shape=outs,
        in_specs=specs,
        out_specs=jax.tree.map(lambda _: place, outs),
        scratch_shapes=scratch,
    )(*args)


def spread(mine, send):
    out = shape(mine.shape, BF16)
    scratch = [pltpu.VMEM(out.shape, BF16), pltpu.SemaphoreType.DMA((8,))]
    chip = call(pair_kernel, out, scratch, mine, near(swap(send)), place=HBM)
    return lax.all_to_all(chip, "y", 0, 0)


def body(
    teacher_hidden,
    proj_weight,
    student_in,
    norm_gain,
    w_query,
    w_keyval,
    w_out,
    row_offsets,
    row_counts,
    doc_start,
):
    tokens_here = teacher_hidden.shape[0]
    quarter = tokens_here // 4
    slots, width = student_in.shape
    high, wide = slots // 4, width // COLS
    core = lax.axis_index("core")
    ypos = lax.axis_index("y")
    core_s = core.astype(jnp.int32).reshape(1)
    start = row_offsets - lax.axis_index("seq") * tokens_here + quarter
    blocks = shape((8, high, wide), BF16)
    parts = shape((8, quarter, wide), BF16)
    goal_mine, goal_send = call(
        goal_kernel,
        (parts, parts),
        [pltpu.VMEM(proj_weight.shape, BF16), pltpu.SemaphoreType.DMA((COLS,))],
        core_s,
        teacher_hidden,
        proj_weight,
        far=1,
    )
    goal_got = spread(goal_mine, goal_send)
    query, keyval, probs, mine, send = pl.pallas_call(
        forward_kernel,
        out_shape=(
            shape((slots, QPK * HD), BF16),
            shape((slots, 2 * HD), BF16),
            shape((QPK, slots, slots), F32),
            blocks,
            blocks,
        ),
        in_specs=[SMEM, VMEM, VMEM, VMEM, HBM, HBM, HBM],
        out_specs=(VMEM,) * 5,
        scratch_shapes=[
            pltpu.VMEM(w_query.shape, BF16),
            pltpu.VMEM(w_keyval.shape, BF16),
            pltpu.VMEM(w_out.shape, BF16),
            pltpu.VMEM((slots, QPK * HD), BF16),
            pltpu.SemaphoreType.DMA((3,)),
        ],
        name="forward",
    )(core_s, student_in, norm_gain, doc_start, w_query, w_keyval, w_out)
    branch_got = spread(mine, send)
    goal_own = jnp.sum(goal_got.astype(F32), axis=0).astype(BF16)
    goal_own = goal_own[None]
    far = jnp.concatenate([turn(goal_own, 3), turn(goal_own, -3)], axis=0)
    below = turn(jnp.concatenate([goal_own, far], axis=0), 1)
    above = turn(jnp.concatenate([goal_own, far[:1]], axis=0), -1)
    ypos_s = ypos.astype(jnp.int32).reshape(1)
    goal_half = call(collect_kernel, parts, (), ypos_s, goal_own, far, near(below), near(above))
    goal_other = swap(goal_half)
    last = jnp.where(core == 1, goal_half[COLS:], goal_other[COLS:])
    earlier = from_behind(last, "seq", 1)
    goal = call(
        align_kernel, shape((slots, width), BF16), (), core_s, start, goal_half, goal_other, earlier
    )
    x_block = lax.dynamic_slice(
        student_in,
        (core * (slots // 2) + (ypos // COLS) * high, (ypos % COLS) * wide),
        (high, wide),
    )
    y_own = call(
        total_kernel,
        blocks,
        [pltpu.VMEM((high, wide), BF16), pltpu.SemaphoreType.DMA((8,))],
        near(branch_got),
        x_block,
        place=HBM,
    )
    y_half = lax.all_to_all(y_own, "y", 0, 0)
    y_other = swap(y_half)
    pieces = shape((8, slots // 16 * (width // HD), HD), BF16)
    saved = (w_out, probs, keyval, query, w_query, w_keyval)
    mine, send = call(
        backward_kernel,
        (pieces, pieces),
        [pltpu.VMEM(a.shape, a.dtype) for a in saved]
        + [
            pltpu.VMEM((slots, width), BF16),
            pltpu.VMEM((slots, (QPK + 2) * HD), BF16),
            pltpu.SemaphoreType.DMA((len(saved),)),
        ],
        core_s,
        row_counts,
        near(y_half),
        near(y_other),
        goal,
        *saved,
        far=len(saved),
    )
    got = spread(mine, send)
    own_rows = slots // 16
    first_row = ((ypos * 2 + core) * own_rows).astype(jnp.int32).reshape(1)
    rows = shape((own_rows, width), F32)
    student_out, dy_own, x_own = call(
        finish_kernel,
        (shape((slots, width), BF16), rows, rows),
        (),
        core_s,
        first_row,
        row_counts,
        y_half,
        y_other,
        goal,
        student_in,
    )
    grad_in = call(
        final_kernel,
        shape((own_rows, width), BF16),
        [pltpu.VMEM((16, width), F32)],
        near(got),
        x_own,
        dy_own,
        norm_gain,
    )
    return (student_out, grad_in)


def solution(mesh):
    seqs, tps = mesh.devices.shape
    split = Mesh(mesh.devices.reshape(seqs, tps // 2, 2), ("seq",) + TP)
    in_specs = (
        P("seq", TP),
        P(TP, None),
        P("seq", None),
        P(),
        P(None, TP),
        P(None, TP),
        P(TP, None),
        P("seq"),
        P("seq"),
        P("seq"),
    )
    out_specs = (P("seq", None), P(("seq",) + TP, None))
    return jax.shard_map(body, mesh=split, in_specs=in_specs, out_specs=out_specs, check_vma=False)
```

```python
import math

import jax
import jax.numpy as jnp
from jax import lax
from jax.experimental import pallas as pl
from jax.experimental.pallas import tpu as pltpu
from jax.sharding import Mesh
from jax.sharding import PartitionSpec as P

HD = 128
QPK = 2
PAIR = [(0, 1), (1, 0)]
COLS = 4
TP = ("y", "core")

epsilon = 1e-06

VMEM = pl.BlockSpec(memory_space=pltpu.VMEM)
SMEM = pl.BlockSpec(memory_space=pltpu.SMEM)
HBM = pl.BlockSpec(memory_space=pltpu.HBM)
F32 = jnp.float32
BF16 = jnp.bfloat16


def near(array):
    return pltpu.with_memory_space_constraint(array, pltpu.VMEM)


def far_off(array):
    return pltpu.with_memory_space_constraint(array, pltpu.HBM)


def shape(dims, dtype):
    return jax.ShapeDtypeStruct(dims, dtype)


def nt(a, b):
    return lax.dot_general(a, b, (((1,), (1,)), ((), ())), preferred_element_type=F32)


def tn(a, b):
    return lax.dot_general(a, b, (((0,), (0,)), ((), ())), preferred_element_type=F32)


def nn(a, b):
    return jnp.dot(a, b, preferred_element_type=F32)


def emit_blocks(core, lhs_ref, weight_ref, mine_ref, send_ref, loads=()):
    half = lhs_ref.shape[0] // 2
    high, wide = mine_ref.shape[1:]
    first = lhs_ref[pl.ds(pl.multiple_of(core * half, 16), half), :]
    second = lhs_ref[pl.ds(pl.multiple_of((1 - core) * half, 16), half), :]
    lhs = jnp.concatenate([first, second], axis=0)
    for j in range(COLS):
        if loads:
            loads[j].wait()
        out = nn(lhs, weight_ref[:, j * wide : (j + 1) * wide])
        for i in range(2):
            mine_ref[i * COLS + j] = out[i * high : (i + 1) * high].astype(BF16)
            send_ref[i * COLS + j] = out[half + i * high : half + (i + 1) * high].astype(BF16)


def goal_kernel(
    core_ref, rows_hbm, weight_hbm, mine_ref, send_ref, rows_ref, weight_ref, sems
):
    wide = mine_ref.shape[2]
    load_rows = pltpu.make_async_copy(rows_hbm, rows_ref, sems.at[COLS])
    load_rows.start()
    loads = []
    for j in range(COLS):
        span = slice(j * wide, (j + 1) * wide)
        load = pltpu.make_async_copy(weight_hbm.at[:, span], weight_ref.at[:, span], sems.at[j])
        load.start()
        loads.append(load)
    load_rows.wait()
    emit_blocks(core_ref[0], rows_ref, weight_ref, mine_ref, send_ref, loads)


def pair_kernel(mine_ref, other_ref, out_hbm, sum_ref, sems):
    stores = []
    for n in range(out_hbm.shape[0]):
        sum_ref[n] = (mine_ref[n].astype(F32) + other_ref[n].astype(F32)).astype(BF16)
        stores.append(pltpu.make_async_copy(sum_ref.at[n], out_hbm.at[n], sems.at[n]))
        stores[n].start()
    for store in stores:
        store.wait()


def align_kernel(start_ref, own_ref, earlier_ref, out_ref):
    slots = out_ref.shape[0]
    wide = own_ref.shape[2]
    row = lax.broadcasted_iota(jnp.int32, (slots, slots), 0)
    col = lax.broadcasted_iota(jnp.int32, (slots, slots), 1)
    pick = (col == row + start_ref[0]).astype(BF16)
    for j in range(COLS):
        bands = [earlier_ref[j]]
        for c in range(2):
            for i in range(2):
                bands.append(own_ref[2 * (i * COLS + j) + c])
        rows = jnp.concatenate(bands, axis=0)
        out_ref[:, j * wide : (j + 1) * wide] = nn(pick, rows).astype(BF16)


def direction(y, t, live, width):
    asum = sum(jnp.sum(a * a, axis=1, keepdims=True) for a in y) + epsilon
    bsum = sum(jnp.sum(a * a, axis=1, keepdims=True) for a in t) + epsilon
    dots = sum(jnp.sum(a * b, axis=1, keepdims=True) for a, b in zip(y, t))
    both = lax.rsqrt(asum * bsum)
    factor = -math.sqrt(width) * live
    return factor * both, factor * (dots * both) / asum


def finish_kernel(
    core_ref, first_ref, count_ref, own_ref, other_ref, goal_ref, x_ref, student_ref, dy_ref, x_own_ref
):
    core = core_ref[0]
    slots, width = student_ref.shape
    high, wide = own_ref.shape[1:]
    for c in range(2):
        for i in range(2):
            first = (2 * c + i) * high
            for j in range(COLS):
                n = i * COLS + j
                block = jnp.where(core == c, own_ref[n].astype(F32), other_ref[n].astype(F32))
                student_ref[first : first + high, j * wide : (j + 1) * wide] = block.astype(BF16)
    own_rows = dy_ref.shape[0]
    row = lax.broadcasted_iota(jnp.int32, (16, slots), 0) + first_ref[0]
    col = lax.broadcasted_iota(jnp.int32, (16, slots), 1)
    pick = (col == row).astype(BF16)
    y = nn(pick, student_ref[...])
    t = nn(pick, goal_ref[...])
    x_own_ref[...] = nn(pick, x_ref[...])[:own_rows]
    place = lax.broadcasted_iota(jnp.int32, (16, 1), 0) + first_ref[0]
    t_scale, y_scale = direction([y], [t], (place < count_ref[0]).astype(F32), width)
    dy_ref[...] = (t * t_scale - y * y_scale)[:own_rows]


def forward_kernel(
    core_ref,
    x_ref,
    gain_ref,
    starts_ref,
    w_query_hbm,
    w_keyval_hbm,
    w_out_hbm,
    query_ref,
    keyval_ref,
    probs_ref,
    mine_ref,
    send_ref,
    w_query,
    w_keyval,
    w_out,
    attn_ref,
    sems,
):
    loads = [
        pltpu.make_async_copy(source, target, sems.at[n])
        for n, (source, target) in enumerate(
            ((w_query_hbm, w_query), (w_keyval_hbm, w_keyval), (w_out_hbm, w_out))
        )
    ]
    for load in loads:
        load.start()
    slots = x_ref.shape[0]
    xf = x_ref[...].astype(F32)
    inv = lax.rsqrt(jnp.mean(xf * xf, axis=1, keepdims=True) + epsilon)
    normed = (xf * inv * gain_ref[...].reshape(1, xf.shape[1])).astype(BF16)
    loads[0].wait()
    query = nn(normed, w_query[...]).astype(BF16)
    query_ref[...] = query
    loads[1].wait()
    keyval = nn(normed, w_keyval[...]).astype(BF16)
    keyval_ref[...] = keyval
    keys = keyval[:, :HD]
    values = keyval[:, HD:]
    row = lax.broadcasted_iota(jnp.int32, (slots, slots), 0)
    col = lax.broadcasted_iota(jnp.int32, (slots, slots), 1)
    across = jnp.where(row == col, starts_ref[...].reshape(1, slots), 0).astype(F32)
    starts = jnp.sum(across, axis=1, keepdims=True).astype(jnp.int32)
    allowed = (col >= starts) & (col <= row)
    for e in range(QPK):
        scores = nt(query[:, e * HD : (e + 1) * HD], keys) * (1.0 / math.sqrt(HD))
        scores = jnp.where(allowed, scores, -jnp.inf)
        expo = jnp.exp(scores - jnp.max(scores, axis=1, keepdims=True))
        probs = expo / jnp.sum(expo, axis=1, keepdims=True)
        probs_ref[e] = probs
        attn_ref[:, e * HD : (e + 1) * HD] = nn(probs.astype(BF16), values).astype(BF16)
    loads[2].wait()
    emit_blocks(core_ref[0], attn_ref, w_out, mine_ref, send_ref)


def total_kernel(got_ref, x_ref, out_hbm, sum_ref, sems):
    branch = got_ref[0].astype(F32)
    for n in range(1, got_ref.shape[0]):
        branch = branch + got_ref[n].astype(F32)
    sum_ref[...] = (x_ref[...].astype(F32) + branch).astype(BF16)
    stores = []
    for n in range(out_hbm.shape[0]):
        stores.append(pltpu.make_async_copy(sum_ref, out_hbm.at[n], sems.at[n]))
        stores[n].start()
    for store in stores:
        store.wait()


def backward_kernel(
    core_ref,
    count_ref,
    own_ref,
    other_ref,
    goal_ref,
    w_out_hbm,
    probs_hbm,
    keyval_hbm,
    query_hbm,
    w_query_hbm,
    w_keyval_hbm,
    mine_ref,
    send_ref,
    w_out,
    probs_ref,
    keyval_ref,
    query_ref,
    w_query,
    w_keyval,
    dyb_ref,
    grads_ref,
    sems,
):
    loads = [
        pltpu.make_async_copy(source, target, sems.at[n])
        for n, (source, target) in enumerate(
            (
                (w_out_hbm, w_out),
                (probs_hbm, probs_ref),
                (keyval_hbm, keyval_ref),
                (query_hbm, query_ref),
                (w_query_hbm, w_query),
                (w_keyval_hbm, w_keyval),
            )
        )
    ]
    for load in loads:
        load.start()
    core = core_ref[0]
    count = count_ref[0]
    slots, width = goal_ref.shape
    high, wide = own_ref.shape[1:]
    for c in range(2):
        for i in range(2):
            first = (2 * c + i) * high
            y, t = [], []
            for j in range(COLS):
                n = i * COLS + j
                y.append(jnp.where(core == c, own_ref[n].astype(F32), other_ref[n].astype(F32)))
                t.append(goal_ref[first : first + high, j * wide : (j + 1) * wide].astype(F32))
            place = lax.broadcasted_iota(jnp.int32, (high, 1), 0) + first
            t_scale, y_scale = direction(y, t, (place < count).astype(F32), width)
            for j in range(COLS):
                dy = t[j] * t_scale - y[j] * y_scale
                dyb_ref[first : first + high, j * wide : (j + 1) * wide] = dy.astype(BF16)
    loads[0].wait()
    d_attn = nt(dyb_ref[...], w_out[...]).astype(BF16)
    for load in loads[1:4]:
        load.wait()
    keys = keyval_ref[:, :HD]
    values = keyval_ref[:, HD:]
    d_keys = d_values = None
    for e in range(QPK):
        head = slice(e * HD, (e + 1) * HD)
        d_out = d_attn[:, head]
        probs = probs_ref[e]
        d_value = tn(probs.astype(BF16), d_out)
        dprob = nt(d_out, values)
        dscore = probs * (dprob - jnp.sum(dprob * probs, axis=1, keepdims=True))
        dscore = (dscore * (1.0 / math.sqrt(HD))).astype(BF16)
        grads_ref[:, head] = nn(dscore, keys).astype(BF16)
        d_key = tn(dscore, query_ref[:, head])
        d_keys = d_key if d_keys is None else d_keys + d_key
        d_values = d_value if d_values is None else d_values + d_value
    grads_ref[:, QPK * HD : (QPK + 1) * HD] = d_keys.astype(BF16)
    grads_ref[:, (QPK + 1) * HD :] = d_values.astype(BF16)
    half = slots // 2
    row = lax.broadcasted_iota(jnp.int32, (slots, slots), 0)
    col = lax.broadcasted_iota(jnp.int32, (slots, slots), 1)
    sent = (row >= half).astype(jnp.int32)
    place = row - half * sent
    parity = core + sent - 2 * core * sent
    late = (place >= 64).astype(jnp.int32)
    early_row = 20 * (place >> 3) + (place & 7)
    late_row = 20 * ((place - 64) >> 1) + 8 + (place & 1)
    source = early_row + late * (late_row - early_row) + 10 * parity
    pick = (col == source).astype(BF16)
    rows = nn(pick, grads_ref[...]).astype(BF16)
    for load in loads[4:]:
        load.wait()
    sub = lax.broadcasted_iota(jnp.int32, (8, HD), 0) >> 1
    for j in range(width // (4 * HD)):
        span = slice(j * 4 * HD, (j + 1) * 4 * HD)
        part = nt(rows[:, : QPK * HD], w_query[span, :]) + nt(rows[:, QPK * HD :], w_keyval[span, :])
        for h, ref in ((0, mine_ref), (1, send_ref)):
            base = h * half
            for k in range(4):
                lane = slice(k * HD, (k + 1) * HD)
                at = 8 * (4 * j + k)
                for n in range(8):
                    ref[n, at : at + 8, :] = part[base + 8 * n : base + 8 * n + 8, lane].astype(BF16)
            for g in range(2):
                low = base + 64 + 8 * g
                tiles = [part[low : low + 8, k * HD : (k + 1) * HD] for k in range(4)]
                for i in range(4):
                    tile = None
                    for k in range(4):
                        turned = pltpu.roll(tiles[k], (2 * k - 2 * i) % 8, 0) if k != i else tiles[k]
                        tile = turned if tile is None else jnp.where(sub == k, turned, tile)
                    at = 224 + 8 * j
                    ref[4 * g + i, at : at + 8, :] = tile.astype(BF16)


def final_kernel(got_ref, x_ref, dy_ref, gain_ref, out_ref, rows_ref):
    total = got_ref[0].astype(F32)
    for n in range(1, got_ref.shape[0]):
        total = total + got_ref[n].astype(F32)
    for t in range(28):
        lane = slice(t * HD, (t + 1) * HD)
        rows_ref[0:8, lane] = total[8 * t : 8 * t + 8]
        at = 224 + 2 * t
        rows_ref[8:10, lane] = total[at : at + 2]
    x = x_ref[...]
    inv = lax.rsqrt(jnp.mean(x * x, axis=1, keepdims=True) + epsilon)
    upper = rows_ref[0:10, :] * gain_ref[...].reshape(1, x.shape[1])
    dx = inv * upper - x * (inv * inv * inv) * jnp.mean(upper * x, axis=1, keepdims=True)
    out_ref[...] = (dy_ref[...] + dx).astype(BF16)


def from_behind(block, axis, distance):
    devices = range(lax.axis_size(axis))
    route = [(i - distance, i) for i in devices if i - distance in devices]
    return lax.ppermute(block, axis, route)


def swap(block):
    return lax.ppermute(block, "core", PAIR)


def call(kernel, outs, scratch, *args, far=0, place=VMEM, limit=None):
    specs = [SMEM if a.shape == (1,) else VMEM for a in args]
    specs[len(args) - far :] = [HBM] * far
    return pl.pallas_call(
        kernel,
        out_shape=outs,
        in_specs=specs,
        out_specs=jax.tree.map(lambda _: place, outs),
        scratch_shapes=scratch,
        compiler_params=pltpu.CompilerParams(vmem_limit_bytes=limit),
    )(*args[: len(args) - far], *map(far_off, args[len(args) - far :]))


def spread(mine, send, kept=True):
    out = shape(mine.shape, BF16)
    first = (near(mine) if kept else mine,)
    scratch = [pltpu.VMEM(out.shape, BF16), pltpu.SemaphoreType.DMA((8,))]
    chip = call(pair_kernel, out, scratch, *first, near(swap(send)), place=HBM)
    return lax.all_to_all(chip, "y", 0, 0)


def body(
    teacher_hidden,
    proj_weight,
    student_in,
    norm_gain,
    w_query,
    w_keyval,
    w_out,
    row_offsets,
    row_counts,
    doc_start,
):
    tokens_here = teacher_hidden.shape[0]
    quarter = tokens_here // 4
    slots, width = student_in.shape
    high, wide = slots // 4, width // COLS
    core = lax.axis_index("core")
    ypos = lax.axis_index("y")
    core_s = core.astype(jnp.int32).reshape(1)
    start = row_offsets - lax.axis_index("seq") * tokens_here + quarter
    blocks = shape((8, high, wide), BF16)
    parts = shape((8, quarter, wide), BF16)
    goal_mine, goal_send = call(
        goal_kernel,
        (parts, parts),
        [
            pltpu.VMEM(teacher_hidden.shape, BF16),
            pltpu.VMEM(proj_weight.shape, BF16),
            pltpu.SemaphoreType.DMA((COLS + 1,)),
        ],
        core_s,
        teacher_hidden,
        proj_weight,
        far=2,
        limit=24 << 20,
    )
    goal_got = spread(goal_mine, goal_send)
    query, keyval, probs, mine, send = pl.pallas_call(
        forward_kernel,
        out_shape=(
            shape((slots, QPK * HD), BF16),
            shape((slots, 2 * HD), BF16),
            shape((QPK, slots, slots), F32),
            blocks,
            blocks,
        ),
        in_specs=[SMEM, VMEM, VMEM, VMEM, HBM, HBM, HBM],
        out_specs=(VMEM,) * 5,
        scratch_shapes=[
            pltpu.VMEM(w_query.shape, BF16),
            pltpu.VMEM(w_keyval.shape, BF16),
            pltpu.VMEM(w_out.shape, BF16),
            pltpu.VMEM((slots, QPK * HD), BF16),
            pltpu.SemaphoreType.DMA((3,)),
        ],
        name="forward",
    )(core_s, student_in, norm_gain, doc_start, w_query, w_keyval, w_out)
    branch_got = spread(mine, send, kept=False)
    goal_own = jnp.sum(goal_got.astype(F32), axis=0).astype(BF16)
    goal_rows = lax.all_gather(goal_own, TP)
    earlier = goal_rows.reshape(2, COLS, 2, quarter, wide)[1, :, 1]
    earlier = from_behind(earlier, "seq", 1)
    goal = call(
        align_kernel, shape((slots, width), BF16), (), start, goal_rows, earlier, limit=24 << 20
    )
    x_block = lax.dynamic_slice(
        student_in,
        (core * (slots // 2) + (ypos // COLS) * high, (ypos % COLS) * wide),
        (high, wide),
    )
    y_own = call(
        total_kernel,
        blocks,
        [pltpu.VMEM((high, wide), BF16), pltpu.SemaphoreType.DMA((8,))],
        near(branch_got),
        x_block,
        place=HBM,
    )
    y_half = lax.all_to_all(y_own, "y", 0, 0)
    y_other = swap(y_half)
    pieces = shape((8, slots // 16 * (width // HD), HD), BF16)
    saved = (w_out, probs, keyval, query, w_query, w_keyval)
    mine, send = call(
        backward_kernel,
        (pieces, pieces),
        [pltpu.VMEM(a.shape, a.dtype) for a in saved]
        + [
            pltpu.VMEM((slots, width), BF16),
            pltpu.VMEM((slots, (QPK + 2) * HD), BF16),
            pltpu.SemaphoreType.DMA((len(saved),)),
        ],
        core_s,
        row_counts,
        near(y_half),
        near(y_other),
        near(goal),
        *saved,
        far=len(saved),
        limit=32 << 20,
    )
    got = spread(mine, send)
    own_rows = slots // 16
    first_row = ((ypos * 2 + core) * own_rows).astype(jnp.int32).reshape(1)
    rows = shape((own_rows, width), F32)
    student_out, dy_own, x_own = call(
        finish_kernel,
        (shape((slots, width), BF16), rows, rows),
        (),
        core_s,
        first_row,
        row_counts,
        y_half,
        y_other,
        goal,
        student_in,
    )
    grad_in = call(
        final_kernel,
        shape((own_rows, width), BF16),
        [pltpu.VMEM((16, width), F32)],
        near(got),
        near(x_own),
        near(dy_own),
        norm_gain,
    )
    return (student_out, grad_in)


def solution(mesh):
    seqs, tps = mesh.devices.shape
    split = Mesh(mesh.devices.reshape(seqs, tps // 2, 2), ("seq",) + TP)
    in_specs = (
        P("seq", TP),
        P(TP, None),
        P("seq", None),
        P(),
        P(None, TP),
        P(None, TP),
        P(TP, None),
        P("seq"),
        P("seq"),
        P("seq"),
    )
    out_specs = (P("seq", None), P(("seq",) + TP, None))
    return jax.shard_map(body, mesh=split, in_specs=in_specs, out_specs=out_specs, check_vma=False)
```

```python
import math

import jax
import jax.numpy as jnp
from jax import lax
from jax.experimental import pallas as pl
from jax.experimental.pallas import tpu as pltpu
from jax.sharding import Mesh
from jax.sharding import PartitionSpec as P

HD = 128
QPK = 2
PAIR = [(0, 1), (1, 0)]
COLS = 4
TP = ("y", "core")

epsilon = 1e-06

VMEM = pl.BlockSpec(memory_space=pltpu.VMEM)
SMEM = pl.BlockSpec(memory_space=pltpu.SMEM)
HBM = pl.BlockSpec(memory_space=pltpu.HBM)
F32 = jnp.float32
BF16 = jnp.bfloat16


def near(array):
    return pltpu.with_memory_space_constraint(array, pltpu.VMEM)


def far_off(array):
    return pltpu.with_memory_space_constraint(array, pltpu.HBM)


def shape(dims, dtype):
    return jax.ShapeDtypeStruct(dims, dtype)


def nt(a, b):
    return lax.dot_general(a, b, (((1,), (1,)), ((), ())), preferred_element_type=F32)


def tn(a, b):
    return lax.dot_general(a, b, (((0,), (0,)), ((), ())), preferred_element_type=F32)


def nn(a, b):
    return jnp.dot(a, b, preferred_element_type=F32)


def emit_blocks(core, lhs_ref, weight_ref, mine_ref, send_ref, loads=()):
    half = lhs_ref.shape[0] // 2
    high, wide = mine_ref.shape[1:]
    first = lhs_ref[pl.ds(pl.multiple_of(core * half, 16), half), :]
    second = lhs_ref[pl.ds(pl.multiple_of((1 - core) * half, 16), half), :]
    lhs = jnp.concatenate([first, second], axis=0)
    for j in range(COLS):
        if loads:
            loads[j].wait()
        out = nn(lhs, weight_ref[:, j * wide : (j + 1) * wide])
        for i in range(2):
            mine_ref[i * COLS + j] = out[i * high : (i + 1) * high].astype(BF16)
            send_ref[i * COLS + j] = out[half + i * high : half + (i + 1) * high].astype(BF16)


def goal_kernel(
    core_ref, rows_hbm, weight_hbm, mine_ref, send_ref, rows_ref, weight_ref, sems
):
    wide = mine_ref.shape[2]
    load_rows = pltpu.make_async_copy(rows_hbm, rows_ref, sems.at[COLS])
    load_rows.start()
    loads = []
    for j in range(COLS):
        span = slice(j * wide, (j + 1) * wide)
        load = pltpu.make_async_copy(weight_hbm.at[:, span], weight_ref.at[:, span], sems.at[j])
        load.start()
        loads.append(load)
    load_rows.wait()
    emit_blocks(core_ref[0], rows_ref, weight_ref, mine_ref, send_ref, loads)


def pair_kernel(mine_ref, other_ref, out_hbm, sum_ref, sems):
    stores = []
    for n in range(out_hbm.shape[0]):
        sum_ref[n] = (mine_ref[n].astype(F32) + other_ref[n].astype(F32)).astype(BF16)
        stores.append(pltpu.make_async_copy(sum_ref.at[n], out_hbm.at[n], sems.at[n]))
        stores[n].start()
    for store in stores:
        store.wait()


def align_kernel(start_ref, own_ref, earlier_ref, out_ref, norm_ref):
    slots = out_ref.shape[0]
    wide = own_ref.shape[2]
    row = lax.broadcasted_iota(jnp.int32, (slots, slots), 0)
    col = lax.broadcasted_iota(jnp.int32, (slots, slots), 1)
    pick = (col == row + start_ref[0]).astype(BF16)
    for j in range(COLS):
        bands = [earlier_ref[j]]
        for c in range(2):
            for i in range(2):
                bands.append(own_ref[2 * (i * COLS + j) + c])
        rows = jnp.concatenate(bands, axis=0)
        goal = nn(pick, rows)
        out_ref[:, j * wide : (j + 1) * wide] = goal.astype(BF16)
        part = jnp.sum(goal * goal, axis=1, keepdims=True)
        bsum = part if j == 0 else bsum + part
    norm_ref[...] = lax.rsqrt(bsum + epsilon)


def direction(y, t, norm, live, width):
    asum = sum(jnp.sum(a * a, axis=1, keepdims=True) for a in y) + epsilon
    dots = sum(jnp.sum(a * b, axis=1, keepdims=True) for a, b in zip(y, t))
    factor = -math.sqrt(width) * live * (lax.rsqrt(asum) * norm)
    return factor, factor * dots / asum


def finish_kernel(
    core_ref, first_ref, count_ref, own_ref, other_ref, goal_ref, x_ref, student_ref, dy_ref, x_own_ref
):
    core = core_ref[0]
    slots, width = student_ref.shape
    high, wide = own_ref.shape[1:]
    for c in range(2):
        for i in range(2):
            first = (2 * c + i) * high
            for j in range(COLS):
                n = i * COLS + j
                block = jnp.where(core == c, own_ref[n].astype(F32), other_ref[n].astype(F32))
                student_ref[first : first + high, j * wide : (j + 1) * wide] = block.astype(BF16)
    own_rows = dy_ref.shape[0]
    row = lax.broadcasted_iota(jnp.int32, (16, slots), 0) + first_ref[0]
    col = lax.broadcasted_iota(jnp.int32, (16, slots), 1)
    pick = (col == row).astype(BF16)
    y = nn(pick, student_ref[...])
    t = nn(pick, goal_ref[...])
    norm = lax.rsqrt(jnp.sum(t * t, axis=1, keepdims=True) + epsilon)
    x_own_ref[...] = nn(pick, x_ref[...])[:own_rows]
    place = lax.broadcasted_iota(jnp.int32, (16, 1), 0) + first_ref[0]
    t_scale, y_scale = direction([y], [t], norm, (place < count_ref[0]).astype(F32), width)
    dy_ref[...] = (t * t_scale - y * y_scale)[:own_rows]


def forward_kernel(
    core_ref,
    x_ref,
    gain_ref,
    starts_ref,
    w_query_hbm,
    w_keyval_hbm,
    w_out_hbm,
    query_ref,
    keyval_ref,
    probs_ref,
    mine_ref,
    send_ref,
    w_query,
    w_keyval,
    w_out,
    attn_ref,
    sems,
):
    loads = [
        pltpu.make_async_copy(source, target, sems.at[n])
        for n, (source, target) in enumerate(
            ((w_query_hbm, w_query), (w_keyval_hbm, w_keyval), (w_out_hbm, w_out))
        )
    ]
    for load in loads:
        load.start()
    slots = x_ref.shape[0]
    xf = x_ref[...].astype(F32)
    inv = lax.rsqrt(jnp.mean(xf * xf, axis=1, keepdims=True) + epsilon)
    normed = (xf * inv * gain_ref[...].reshape(1, xf.shape[1])).astype(BF16)
    loads[0].wait()
    query = nn(normed, w_query[...]).astype(BF16)
    query_ref[...] = query
    loads[1].wait()
    keyval = nn(normed, w_keyval[...]).astype(BF16)
    keyval_ref[...] = keyval
    keys = keyval[:, :HD]
    values = keyval[:, HD:]
    row = lax.broadcasted_iota(jnp.int32, (slots, slots), 0)
    col = lax.broadcasted_iota(jnp.int32, (slots, slots), 1)
    across = jnp.where(row == col, starts_ref[...].reshape(1, slots), 0).astype(F32)
    starts = jnp.sum(across, axis=1, keepdims=True).astype(jnp.int32)
    allowed = (col >= starts) & (col <= row)
    for e in range(QPK):
        scores = nt(query[:, e * HD : (e + 1) * HD], keys) * (1.0 / math.sqrt(HD))
        scores = jnp.where(allowed, scores, -jnp.inf)
        expo = jnp.exp(scores - jnp.max(scores, axis=1, keepdims=True))
        probs = expo / jnp.sum(expo, axis=1, keepdims=True)
        probs_ref[e] = probs
        attn_ref[:, e * HD : (e + 1) * HD] = nn(probs.astype(BF16), values).astype(BF16)
    loads[2].wait()
    emit_blocks(core_ref[0], attn_ref, w_out, mine_ref, send_ref)


def total_kernel(got_ref, x_ref, out_hbm, sum_ref, sems):
    branch = got_ref[0].astype(F32)
    for n in range(1, got_ref.shape[0]):
        branch = branch + got_ref[n].astype(F32)
    sum_ref[...] = (x_ref[...].astype(F32) + branch).astype(BF16)
    stores = []
    for n in range(out_hbm.shape[0]):
        stores.append(pltpu.make_async_copy(sum_ref, out_hbm.at[n], sems.at[n]))
        stores[n].start()
    for store in stores:
        store.wait()


def backward_kernel(
    core_ref,
    count_ref,
    own_ref,
    other_ref,
    goal_ref,
    norm_ref,
    w_out_hbm,
    probs_hbm,
    keyval_hbm,
    query_hbm,
    w_query_hbm,
    w_keyval_hbm,
    mine_ref,
    send_ref,
    w_out,
    probs_ref,
    keyval_ref,
    query_ref,
    w_query,
    w_keyval,
    dyb_ref,
    grads_ref,
    d_attn_ref,
    sems,
):
    loads = [
        pltpu.make_async_copy(source, target, sems.at[n])
        for n, (source, target) in enumerate(
            (
                (w_out_hbm, w_out),
                (probs_hbm, probs_ref),
                (keyval_hbm, keyval_ref),
                (query_hbm, query_ref),
                (w_query_hbm, w_query),
                (w_keyval_hbm, w_keyval),
            )
        )
    ]
    for load in loads:
        load.start()
    core = core_ref[0]
    count = count_ref[0]
    slots, width = goal_ref.shape
    high, wide = own_ref.shape[1:]
    half = slots // 2
    for c, ref in ((0, own_ref), (1, other_ref)):
        base = pl.multiple_of((core if c == 0 else 1 - core) * half, 16)
        for i in range(2):
            rows = pl.ds(pl.multiple_of(base + i * high, 8), high)
            y = [ref[i * COLS + j].astype(F32) for j in range(COLS)]
            t = [goal_ref[rows, j * wide : (j + 1) * wide].astype(F32) for j in range(COLS)]
            place = lax.broadcasted_iota(jnp.int32, (high, 1), 0) + base + i * high
            live = (place < count).astype(F32)
            to_t, to_y = direction(y, t, norm_ref[rows, :], live, width)
            first = c * half + i * high
            for j in range(COLS):
                dy = t[j] * to_t - y[j] * to_y
                dyb_ref[first : first + high, j * wide : (j + 1) * wide] = dy.astype(BF16)
    loads[0].wait()
    d_rows = nt(dyb_ref[...], w_out[...]).astype(BF16)
    d_attn_ref[pl.ds(pl.multiple_of(core * half, 16), half), :] = d_rows[:half]
    d_attn_ref[pl.ds(pl.multiple_of((1 - core) * half, 16), half), :] = d_rows[half:]
    d_attn = d_attn_ref[...]
    for load in loads[1:4]:
        load.wait()
    keys = keyval_ref[:, :HD]
    values = keyval_ref[:, HD:]
    d_keys = d_values = None
    for e in range(QPK):
        head = slice(e * HD, (e + 1) * HD)
        d_out = d_attn[:, head]
        probs = probs_ref[e]
        d_value = tn(probs.astype(BF16), d_out)
        dprob = nt(d_out, values)
        dscore = probs * (dprob - jnp.sum(dprob * probs, axis=1, keepdims=True))
        dscore = (dscore * (1.0 / math.sqrt(HD))).astype(BF16)
        grads_ref[:, head] = nn(dscore, keys).astype(BF16)
        d_key = tn(dscore, query_ref[:, head])
        d_keys = d_key if d_keys is None else d_keys + d_key
        d_values = d_value if d_values is None else d_values + d_value
    grads_ref[:, QPK * HD : (QPK + 1) * HD] = d_keys.astype(BF16)
    grads_ref[:, (QPK + 1) * HD :] = d_values.astype(BF16)
    row = lax.broadcasted_iota(jnp.int32, (slots, slots), 0)
    col = lax.broadcasted_iota(jnp.int32, (slots, slots), 1)
    sent = (row >= half).astype(jnp.int32)
    place = row - half * sent
    parity = core + sent - 2 * core * sent
    late = (place >= 64).astype(jnp.int32)
    early_row = 20 * (place >> 3) + (place & 7)
    late_row = 20 * ((place - 64) >> 1) + 8 + (place & 1)
    source = early_row + late * (late_row - early_row) + 10 * parity
    pick = (col == source).astype(BF16)
    rows = nn(pick, grads_ref[...]).astype(BF16)
    for load in loads[4:]:
        load.wait()
    sub = lax.broadcasted_iota(jnp.int32, (8, HD), 0) >> 1
    for j in range(width // (4 * HD)):
        span = slice(j * 4 * HD, (j + 1) * 4 * HD)
        part = nt(rows[:, : QPK * HD], w_query[span, :]) + nt(rows[:, QPK * HD :], w_keyval[span, :])
        for h, ref in ((0, mine_ref), (1, send_ref)):
            base = h * half
            for k in range(4):
                lane = slice(k * HD, (k + 1) * HD)
                at = 8 * (4 * j + k)
                for n in range(8):
                    ref[n, at : at + 8, :] = part[base + 8 * n : base + 8 * n + 8, lane].astype(BF16)
            for g in range(2):
                low = base + 64 + 8 * g
                tiles = [part[low : low + 8, k * HD : (k + 1) * HD] for k in range(4)]
                for i in range(4):
                    tile = None
                    for k in range(4):
                        turned = pltpu.roll(tiles[k], (2 * k - 2 * i) % 8, 0) if k != i else tiles[k]
                        tile = turned if tile is None else jnp.where(sub == k, turned, tile)
                    at = 224 + 8 * j
                    ref[4 * g + i, at : at + 8, :] = tile.astype(BF16)


def final_kernel(got_ref, x_ref, dy_ref, gain_ref, out_ref, rows_ref):
    total = got_ref[0].astype(F32)
    for n in range(1, got_ref.shape[0]):
        total = total + got_ref[n].astype(F32)
    for t in range(28):
        lane = slice(t * HD, (t + 1) * HD)
        rows_ref[0:8, lane] = total[8 * t : 8 * t + 8]
        at = 224 + 2 * t
        rows_ref[8:10, lane] = total[at : at + 2]
    x = x_ref[...]
    inv = lax.rsqrt(jnp.mean(x * x, axis=1, keepdims=True) + epsilon)
    upper = rows_ref[0:10, :] * gain_ref[...].reshape(1, x.shape[1])
    dx = inv * upper - x * (inv * inv * inv) * jnp.mean(upper * x, axis=1, keepdims=True)
    out_ref[...] = (dy_ref[...] + dx).astype(BF16)


def from_behind(block, axis, distance):
    devices = range(lax.axis_size(axis))
    route = [(i - distance, i) for i in devices if i - distance in devices]
    return lax.ppermute(block, axis, route)


def swap(block):
    return lax.ppermute(block, "core", PAIR)


def call(kernel, outs, scratch, *args, far=0, place=VMEM, limit=None):
    specs = [SMEM if a.shape == (1,) else VMEM for a in args]
    specs[len(args) - far :] = [HBM] * far
    return pl.pallas_call(
        kernel,
        out_shape=outs,
        in_specs=specs,
        out_specs=jax.tree.map(lambda _: place, outs),
        scratch_shapes=scratch,
        compiler_params=pltpu.CompilerParams(vmem_limit_bytes=limit),
    )(*args[: len(args) - far], *map(far_off, args[len(args) - far :]))


def spread(mine, send, kept=True):
    out = shape(mine.shape, BF16)
    first = (near(mine) if kept else mine,)
    scratch = [pltpu.VMEM(out.shape, BF16), pltpu.SemaphoreType.DMA((8,))]
    chip = call(pair_kernel, out, scratch, *first, near(swap(send)), place=HBM)
    return lax.all_to_all(chip, "y", 0, 0)


def body(
    teacher_hidden,
    proj_weight,
    student_in,
    norm_gain,
    w_query,
    w_keyval,
    w_out,
    row_offsets,
    row_counts,
    doc_start,
):
    tokens_here = teacher_hidden.shape[0]
    quarter = tokens_here // 4
    slots, width = student_in.shape
    high, wide = slots // 4, width // COLS
    core = lax.axis_index("core")
    ypos = lax.axis_index("y")
    core_s = core.astype(jnp.int32).reshape(1)
    start = row_offsets - lax.axis_index("seq") * tokens_here + quarter
    blocks = shape((8, high, wide), BF16)
    parts = shape((8, quarter, wide), BF16)
    goal_mine, goal_send = call(
        goal_kernel,
        (parts, parts),
        [
            pltpu.VMEM(teacher_hidden.shape, BF16),
            pltpu.VMEM(proj_weight.shape, BF16),
            pltpu.SemaphoreType.DMA((COLS + 1,)),
        ],
        core_s,
        teacher_hidden,
        proj_weight,
        far=2,
        limit=24 << 20,
    )
    goal_got = spread(goal_mine, goal_send)
    query, keyval, probs, mine, send = pl.pallas_call(
        forward_kernel,
        out_shape=(
            shape((slots, QPK * HD), BF16),
            shape((slots, 2 * HD), BF16),
            shape((QPK, slots, slots), F32),
            blocks,
            blocks,
        ),
        in_specs=[SMEM, VMEM, VMEM, VMEM, HBM, HBM, HBM],
        out_specs=(VMEM,) * 5,
        scratch_shapes=[
            pltpu.VMEM(w_query.shape, BF16),
            pltpu.VMEM(w_keyval.shape, BF16),
            pltpu.VMEM(w_out.shape, BF16),
            pltpu.VMEM((slots, QPK * HD), BF16),
            pltpu.SemaphoreType.DMA((3,)),
        ],
        name="forward",
    )(core_s, student_in, norm_gain, doc_start, w_query, w_keyval, w_out)
    branch_got = spread(mine, send, kept=False)
    goal_own = jnp.sum(goal_got.astype(F32), axis=0).astype(BF16)
    goal_rows = lax.all_gather(goal_own, TP)
    earlier = goal_rows.reshape(2, COLS, 2, quarter, wide)[1, :, 1]
    earlier = from_behind(earlier, "seq", 1)
    goal, norm = call(
        align_kernel,
        (shape((slots, width), BF16), shape((slots, 1), F32)),
        (),
        start,
        goal_rows,
        earlier,
        limit=24 << 20,
    )
    x_block = lax.dynamic_slice(
        student_in,
        (core * (slots // 2) + (ypos // COLS) * high, (ypos % COLS) * wide),
        (high, wide),
    )
    y_own = call(
        total_kernel,
        blocks,
        [pltpu.VMEM((high, wide), BF16), pltpu.SemaphoreType.DMA((8,))],
        near(branch_got),
        x_block,
        place=HBM,
    )
    y_half = lax.all_to_all(y_own, "y", 0, 0)
    y_other = swap(y_half)
    pieces = shape((8, slots // 16 * (width // HD), HD), BF16)
    saved = (w_out, probs, keyval, query, w_query, w_keyval)
    mine, send = call(
        backward_kernel,
        (pieces, pieces),
        [pltpu.VMEM(a.shape, a.dtype) for a in saved]
        + [
            pltpu.VMEM((slots, width), BF16),
            pltpu.VMEM((slots, (QPK + 2) * HD), BF16),
            pltpu.VMEM((slots, QPK * HD), BF16),
            pltpu.SemaphoreType.DMA((len(saved),)),
        ],
        core_s,
        row_counts,
        near(y_half),
        near(y_other),
        near(goal),
        norm,
        *saved,
        far=len(saved),
        limit=32 << 20,
    )
    got = spread(mine, send)
    own_rows = slots // 16
    first_row = ((ypos * 2 + core) * own_rows).astype(jnp.int32).reshape(1)
    rows = shape((own_rows, width), F32)
    student_out, dy_own, x_own = call(
        finish_kernel,
        (shape((slots, width), BF16), rows, rows),
        (),
        core_s,
        first_row,
        row_counts,
        y_half,
        y_other,
        goal,
        student_in,
    )
    grad_in = call(
        final_kernel,
        shape((own_rows, width), BF16),
        [pltpu.VMEM((16, width), F32)],
        near(got),
        x_own,
        dy_own,
        norm_gain,
    )
    return (student_out, grad_in)


def solution(mesh):
    seqs, tps = mesh.devices.shape
    split = Mesh(mesh.devices.reshape(seqs, tps // 2, 2), ("seq",) + TP)
    in_specs = (
        P("seq", TP),
        P(TP, None),
        P("seq", None),
        P(),
        P(None, TP),
        P(None, TP),
        P(TP, None),
        P("seq"),
        P("seq"),
        P("seq"),
    )
    out_specs = (P("seq", None), P(("seq",) + TP, None))
    return jax.shard_map(body, mesh=split, in_specs=in_specs, out_specs=out_specs, check_vma=False)
```
